128 devices in a mesh: grp: 2 (over y_hi), row: 8 (over z, y_lo), col: 8 (over x, core).
Axes of the slice: x: 4, y: 4 (y_hi: 2, y_lo: 2; y = y_hi * 2 + y_lo), z: 4, core: 2. Of those that a mesh axis runs over, the one named last changes fastest.
Arguments:
- queries: bfloat16 [8192, 2048], P(('row', 'col'), 'grp'), parts along dimension 1, may hold values from -102 to 102
- keys: bfloat16 [8192, 256], P(('col', 'row'), 'grp'), parts along dimension 1, may hold values from -5 to 5
- values: bfloat16 [8192, 256], P(('col', 'row'), 'grp'), parts along dimension 1, may hold values from -6 to 6
- span_order: int32 [64], replicated, may hold values from 0 to 63, each once
Outputs:
- attended: float32 [8192, 2048], P(('row', 'col'), 'grp'), parts along dimension 1
The draws below stay inside these ranges and needn't reach their ends.
There are 2 independent parts, one for each index of `grp`. The reference program is written for one: setup_inputs(seed, part) draws one part's arguments, and reference() takes and returns one part's arrays. A program takes and returns all parts, laid end to end along the dimension named above; an argument that names none is the same for every part. Nothing has to cross between parts.
All inputs are finite; a program needn't handle non-finite values.
Results may differ from the reference program's by a relative error of at most 0.0022.
Values may be sent and summed in bfloat16 or wider, within the bound.
No kernel may reach another device: no remote copies, remote signals or barrier semaphores. Data moves between devices by JAX's collectives and lax.ppermute only.
A program may use at most 64 MiB of HBM per device.

```python
import math
import jax
import jax.numpy as jnp
from jax import lax

HEADS = 8
HD = 128
SPAN = 128
SEQ = 8192
NCH = 64
N_ROW = 8
N_COL = 8


def shared_draw(key):
    keys_raw = jnp.clip(jax.random.normal(jax.random.fold_in(key, 101), (SEQ, HD), jnp.float32), -5.0, 5.0)
    queries_raw = jnp.clip(jax.random.normal(jax.random.fold_in(key, 102), (SEQ, HEADS * HD), jnp.float32), -5.0, 5.0)
    return (queries_raw, keys_raw)


def draw_queries(key, part):
    return shared_draw(key)[0].astype(jnp.bfloat16)


def draw_keys(key, part):
    return shared_draw(key)[1].astype(jnp.bfloat16)


def block_scale(key, shape, pieces, smallest, largest):
    level, own = 1.0, jax.random.fold_in(key, 6)
    for axis_at, shards_of in pieces:
        draws = jnp.exp(jax.random.uniform(jax.random.fold_in(own, axis_at), (shards_of,), jnp.float32, smallest / len(pieces), largest / len(pieces)))
        level = level * jnp.repeat(draws, shape[axis_at] // shards_of).reshape([-1 if axis == axis_at else 1 for axis in range(len(shape))])
    return level


def gaussian(own_key, dims, spread, bound, shards=(), held_as=jnp.bfloat16):
    array = jax.random.normal(own_key, dims, jnp.float32) * spread
    if len(shards) > 0:
        array = block_scale(own_key, dims, shards, -0.22, 0.18) * array
    return jnp.clip(array, min=-bound, max=bound).astype(held_as)


def setup_inputs(seed: int = 0, part: int = 0) -> dict:
    key_list = jax.random.split(jax.random.key(seed), 5)
    own_keys = jax.random.split(jax.random.fold_in(key_list[4], part), 5)
    return {
        "queries": draw_queries(jax.random.fold_in(jax.random.fold_in(key_list[4], part), 71), part),
        "keys": draw_keys(jax.random.fold_in(jax.random.fold_in(key_list[4], part), 71), part),
        "values": gaussian(own_keys[2], (SEQ, HD), 1.0, 6.0, ((0, 64),)),
        "span_order": jax.random.permutation(key_list[3], NCH).astype(jnp.int32),
    }


def span_positions(span_order, indices):
    return span_order[indices // SPAN] * SPAN + indices % SPAN

def block_partial(query_blk, query_pos, key_blk, value_blk, key_pos):
    scores = jnp.einsum('bhd,nd->bhn', query_blk.astype(jnp.float32), key_blk.astype(jnp.float32)) * (1.0 / math.sqrt(HD))
    allowed = query_pos[:, None, None] >= key_pos[None, None, :]
    scores = jnp.where(allowed, scores, -1e+30)
    row_max = lax.optimization_barrier(jnp.max(scores, axis=2))
    weights = jnp.where(allowed, jnp.exp(scores - row_max[..., None]), 0.0)
    totals = lax.optimization_barrier(jnp.sum(weights, axis=2))
    rounded = weights.astype(jnp.bfloat16)
    summed = jnp.einsum('bhn,nd->bhd', rounded.astype(jnp.float32), value_blk.astype(jnp.float32))
    live = totals > 0
    safe = jnp.where(live, totals, 1.0)
    partial_value = jnp.where(live[..., None], summed / safe[..., None], 0.0)
    lse = jnp.where(live, row_max + jnp.log(safe), -1e+30)
    return (partial_value.reshape(partial_value.shape[0], HEADS * HD), lse)

def combine_flat(partials, lses):
    count = partials.shape[0]
    rows_here = partials.shape[1]
    best = lax.optimization_barrier(jnp.max(lses, axis=0))
    scales = jnp.exp(lses - best[None])
    outs = partials.reshape(count, rows_here, HEADS, HD)
    numer = lax.optimization_barrier(jnp.sum(scales[..., None] * outs, axis=0))
    denom = lax.optimization_barrier(jnp.sum(scales, axis=0))
    return (numer / denom[..., None]).reshape(rows_here, HEADS * HD)

def reference(queries, keys, values, span_order):
    position = span_positions(span_order, jnp.arange(SEQ, dtype=jnp.int32))
    row_len = SEQ // N_ROW
    col_len = SEQ // N_COL
    query_blocks = queries.reshape(N_ROW, row_len, HEADS, HD)
    query_posb = position.reshape(N_ROW, row_len)
    key_blocks = keys.reshape(N_COL, col_len, HD)
    value_blocks = values.reshape(N_COL, col_len, HD)
    key_posb = position.reshape(N_COL, col_len)

    def one_row(pair):
        query_blk, query_pos = pair

        def one_col(triple):
            return block_partial(query_blk, query_pos, triple[0], triple[1], triple[2])
        partials, lses = lax.map(one_col, (key_blocks, value_blocks, key_posb))
        return combine_flat(partials, lses)
    result = lax.map(one_row, (query_blocks, query_posb))
    return result.reshape(SEQ, HEADS * HD)
```

```python
import functools
import math

import jax
import jax.numpy as jnp
from jax import lax
from jax.experimental import pallas as pl
from jax.experimental.pallas import tpu as pltpu
from jax.sharding import PartitionSpec as P

HEADS = 8
HD = 128
SPAN = 128
ROWS = HEADS * SPAN
GROUP = 4
BLOCK = GROUP * SPAN
NEVER = -1e30
SCALE = math.log2(math.e) / math.sqrt(HD)
VMEM = pltpu.VMEM
AXES = ("row", "col")


def place(z, y, x, core):
    return (z % 4 * 2 + y % 2) * 8 + x % 4 * 2 + core


def coords(index):
    row, col = divmod(index, 8)
    return row // 2, row % 2, col // 2, col % 2


def moved(to):
    return [(i, place(*to(*coords(i)))) for i in range(64)]


def along_a(step):
    return moved(lambda z, y, x, c: (z + step, y, x, c) if c == 0 else (z, y, x + step, c))


def along_b(step):
    return moved(lambda z, y, x, c: (z, y, x + step, c) if c == 0 else (z + step, y, x, c))


ACROSS_Y = moved(lambda z, y, x, c: (z, 1 - y, x, c))
ACROSS_CORE = moved(lambda z, y, x, c: (z, y, x, 1 - c))


def send(x, perm):
    return lax.ppermute(x, AXES, perm)


def whole(space=VMEM):
    return pl.BlockSpec(memory_space=space)


def split_queries(q_ref, out_ref):
    for head in range(HEADS):
        q = q_ref[:, head * HD : (head + 1) * HD].astype(jnp.float32) * SCALE
        high = q.astype(jnp.bfloat16)
        low = (q - high.astype(jnp.float32)).astype(jnp.bfloat16)
        out_ref[head * SPAN : (head + 1) * SPAN, :] = jnp.concatenate([high, low], axis=1)


def prepared(queries):
    return pl.pallas_call(
        split_queries,
        out_shape=jax.ShapeDtypeStruct((ROWS, 2 * HD), jnp.bfloat16),
        in_specs=[whole()],
        out_specs=whole(),
        name="prepare",
        cost_estimate=pl.CostEstimate(flops=4 * ROWS * HD, bytes_accessed=6 * ROWS * HD, transcendentals=0),
    )(queries)


def chunk_kernel(who, slots, arrays, first, *refs):
    order_ref, q_ref, *refs = refs
    kv_refs, refs = refs[:arrays], refs[arrays:]
    if not first:
        m_in, acc_in, *refs = refs
    m_ref, acc_ref, kv_ref, s_ref, list_ref, kind_ref = refs

    row, col = lax.axis_index("row"), lax.axis_index("col")
    z, y, x, core = row // 2, row % 2, col // 2, col % 2
    on_z = (core == 0).astype(jnp.int32)

    def order_of(offset):
        da, dy, db = offset
        sz = (z + on_z * da + (1 - on_z) * db + 4) % 4
        sx = (x + on_z * db + (1 - on_z) * da + 4) % 4
        sy = (y + dy) % 2
        return order_ref[(sx * 2 + core) * 8 + sz * 2 + sy]

    for slot, (array, at, _) in enumerate(slots):
        kv_ref[slot] = kv_refs[array][at * SPAN : (at + 1) * SPAN, :]
    key_orders = [order_of(offset) for _, _, offset in slots]
    steps = []
    for u, other in enumerate(who):
        mine = order_ref[row * 8 + x * 2 + (1 - core if other else core)]
        used = jnp.int32(0)
        for slot, theirs in enumerate(key_orders):
            list_ref[u, used] = slot
            kind_ref[u, used] = jnp.where(theirs == mine, 0, -SPAN)
            used = used + (theirs <= mine).astype(jnp.int32)
        for extra in range(GROUP - 1):
            list_ref[u, used + extra] = 0
            kind_ref[u, used + extra] = SPAN
        steps.append((used + GROUP - 1) // GROUP)
    before = steps[0]
    total = functools.reduce(lambda a, b: a + b, steps)

    for u, other in enumerate(who):
        here = slice(u * ROWS, (u + 1) * ROWS)
        there = slice(other * ROWS, (other + 1) * ROWS)
        if first:
            m_ref[here, :] = jnp.full((ROWS, HD), NEVER, jnp.float32)
            acc_ref[here, :] = jnp.zeros((ROWS, 2 * HD), jnp.float32)
        else:
            m_ref[here, :] = m_in[there, :]
            acc_ref[here, :] = acc_in[there, :]

    above = lax.broadcasted_iota(jnp.int32, (SPAN, SPAN), 0) - lax.broadcasted_iota(jnp.int32, (SPAN, SPAN), 1)

    def where_of(step):
        u = (step >= before).astype(jnp.int32)
        return u, (step - u * before) * GROUP

    def rows_of(u):
        return pl.ds(pl.multiple_of(u * ROWS, ROWS), ROWS)

    def score(step, half):
        u, at = where_of(step)
        q_at = u if len(who) == 2 else who[0]
        k = jnp.concatenate([kv_ref[list_ref[u, at + g], :, :HD] for g in range(GROUP)], axis=0)
        s = lax.dot_general(
            q_ref[rows_of(q_at), :],
            jnp.concatenate([k, k], axis=1),
            (((1,), (1,)), ((), ())),
            preferred_element_type=jnp.float32,
        )
        tiles = []
        for g in range(GROUP):
            allowed = above >= kind_ref[u, at + g]
            tile = s[:, g * SPAN : (g + 1) * SPAN].reshape(HEADS, SPAN, SPAN)
            tiles.append(jnp.where(allowed[None], tile, NEVER).reshape(ROWS, SPAN))
        s = jnp.concatenate(tiles, axis=1)
        s_ref[half] = s
        return jnp.max(s, axis=1, keepdims=True)

    def absorb(step, half, top):
        u, at = where_of(step)
        rows = rows_of(u)
        old = m_ref[rows, :]
        new = jnp.maximum(old, top)
        fade = jnp.exp2(old - new)
        m_ref[rows, :] = new
        weights = jnp.exp2(s_ref[half] - jnp.concatenate([new] * GROUP, axis=1)).astype(jnp.bfloat16)
        v = jnp.concatenate([kv_ref[list_ref[u, at + g], :, HD:] for g in range(GROUP)], axis=0)
        v = jnp.concatenate([v, jnp.ones((BLOCK, HD), jnp.bfloat16)], axis=1)
        more = jnp.dot(weights, v, preferred_element_type=jnp.float32)
        acc_ref[rows, :] = acc_ref[rows, :] * jnp.concatenate([fade, fade], axis=1) + more

    @pl.when(total > 0)
    def _():
        top = score(0, 0)

        def two(pair, top):
            step = 2 * pair
            later = score(step + 1, 1)
            absorb(step, 0, top)
            top = score(jnp.minimum(step + 2, total - 1), 0)
            absorb(step + 1, 1, later)
            return top

        top = lax.fori_loop(0, total // 2, two, top)

        @pl.when(total % 2 == 1)
        def _():
            absorb(total - 1, 0, top)


def attend(name, who, slots, span_order, queries, arrays, state=None):
    users = len(who)
    rows = users * ROWS
    tiles = users * len(slots)
    out = [jax.ShapeDtypeStruct((rows, HD), jnp.float32), jax.ShapeDtypeStruct((rows, 2 * HD), jnp.float32)]
    held = [] if state is None else list(state)
    return pl.pallas_call(
        functools.partial(chunk_kernel, who, slots, len(arrays), state is None),
        out_shape=out,
        in_specs=[whole(pltpu.SMEM)] + [whole()] * (1 + len(arrays) + len(held)),
        out_specs=[whole(), whole()],
        scratch_shapes=[
            VMEM((len(slots), SPAN, 2 * HD), jnp.bfloat16),
            VMEM((2, ROWS, BLOCK), jnp.float32),
            pltpu.SMEM((users, len(slots) + GROUP), jnp.int32),
            pltpu.SMEM((users, len(slots) + GROUP), jnp.int32),
        ],
        compiler_params=pltpu.CompilerParams(vmem_limit_bytes=32 << 20),
        cost_estimate=pl.CostEstimate(
            flops=4 * tiles * ROWS * SPAN * HD,
            bytes_accessed=tiles * SPAN * SPAN * 4,
            transcendentals=tiles * ROWS * SPAN,
        ),
        name=name,
    )(span_order, queries, *arrays, *held)


def merge_kernel(m_ref, acc_ref, far_m_ref, far_acc_ref, out_ref):
    for head in range(HEADS):
        rows = slice(head * SPAN, (head + 1) * SPAN)
        near, far = m_ref[rows, :], far_m_ref[rows, :]
        top = jnp.maximum(near, far)
        near, far = jnp.exp2(near - top), jnp.exp2(far - top)
        value = acc_ref[rows, :HD] * near + far_acc_ref[rows, :HD] * far
        weight = acc_ref[rows, HD:] * near + far_acc_ref[rows, HD:] * far
        out_ref[:, head * HD : (head + 1) * HD] = value / weight


def merged(near, far):
    return pl.pallas_call(
        merge_kernel,
        out_shape=jax.ShapeDtypeStruct((SPAN, HEADS * HD), jnp.float32),
        in_specs=[whole()] * 4,
        out_specs=whole(),
        name="merge",
        cost_estimate=pl.CostEstimate(flops=8 * ROWS * HD, bytes_accessed=28 * ROWS * HD, transcendentals=2 * ROWS * HD),
    )(*near, *far)


NEAR_A = (0, -1, 1, 2)
FAR_B = (-1, 1, 2)


def local(queries, keys, values, span_order):
    kv = jnp.concatenate([keys, values], axis=1)
    by_y = send(kv, ACROSS_Y)
    by_a = [send(kv, along_a(-d)) for d in NEAR_A[1:]]
    partner = send(queries, ACROSS_CORE)
    split = jnp.concatenate([prepared(queries), prepared(partner)], axis=0)

    beside = jnp.concatenate(by_a, axis=0)
    plane = jnp.concatenate([kv, beside], axis=0)
    by_ya = send(beside, ACROSS_Y)
    by_b = [send(plane, along_b(-d)) for d in FAR_B]
    slots = tuple((0, k, (a, 0, 0)) for k, a in enumerate(NEAR_A))
    state = attend("near", (0, 1), slots, span_order, split, [plane])

    other = jnp.concatenate([by_y, by_ya], axis=0)
    by_yb = [send(other, along_b(-d)) for d in FAR_B]
    slots = tuple((0, k, (a, 1, 0)) for k, a in enumerate(NEAR_A))
    state = attend("near_y", (0, 1), slots, span_order, split, [other], state)

    slots = tuple((j, k, (a, 0, b)) for j, b in enumerate(FAR_B) for k, a in enumerate(NEAR_A))
    state = attend("far", (0, 1), slots, span_order, split, by_b, state)

    slots = tuple((j, k, (a, 1, b)) for j, b in enumerate(FAR_B) for k, a in enumerate(NEAR_A))
    theirs = attend("far_y_partner", (1,), slots, span_order, split, by_yb, state)
    away = [send(part, ACROSS_CORE) for part in theirs]
    mine = attend("far_y_own", (0,), slots, span_order, split, by_yb, state)
    return merged(mine, away)


def solution(mesh):
    placed = (P(("row", "col"), "grp"), P(("col", "row"), "grp"), P(("col", "row"), "grp"), P())
    return jax.shard_map(
        local, mesh=mesh, in_specs=placed, out_specs=P(("row", "col"), "grp"), check_vma=False
    )
```

```python
import functools
import math

import jax
import jax.numpy as jnp
from jax import lax
from jax.experimental import pallas as pl
from jax.experimental.pallas import tpu as pltpu
from jax.sharding import PartitionSpec as P

HEADS = 8
HD = 128
SPAN = 128
ROWS = HEADS * SPAN
GROUP = 4
BLOCK = GROUP * SPAN
NEVER = -1e30
SCALE = math.log2(math.e) / math.sqrt(HD)
VMEM = pltpu.VMEM
AXES = ("row", "col")


def place(z, y, x, core):
    return (z % 4 * 2 + y % 2) * 8 + x % 4 * 2 + core


def coords(index):
    row, col = divmod(index, 8)
    return row // 2, row % 2, col // 2, col % 2


def moved(to):
    return [(i, place(*to(*coords(i)))) for i in range(64)]


def along_a(step):
    return moved(lambda z, y, x, c: (z + step, y, x, c) if c == 0 else (z, y, x + step, c))


def along_b(step):
    return moved(lambda z, y, x, c: (z, y, x + step, c) if c == 0 else (z + step, y, x, c))


ACROSS_Y = moved(lambda z, y, x, c: (z, 1 - y, x, c))
ACROSS_CORE = moved(lambda z, y, x, c: (z, y, x, 1 - c))

def send(x, perm):
    return lax.ppermute(x, AXES, perm)


def whole(space=VMEM):
    return pl.BlockSpec(memory_space=space)


def limit(mib):
    return pltpu.CompilerParams(vmem_limit_bytes=mib << 20)


def cost(flops, moved_bytes, exps=0):
    return pl.CostEstimate(flops=flops, bytes_accessed=moved_bytes, transcendentals=exps)


def pack_kernel(k_ref, v_ref, out_ref, done):
    copies = [
        pltpu.make_async_copy(k_ref, out_ref.at[:, :HD], done.at[0]),
        pltpu.make_async_copy(v_ref, out_ref.at[:, HD:], done.at[1]),
    ]
    for copy in copies:
        copy.start()
    for copy in copies:
        copy.wait()


def packed(keys, values):
    return pl.pallas_call(
        pack_kernel,
        out_shape=jax.ShapeDtypeStruct((SPAN, 2 * HD), jnp.bfloat16),
        in_specs=[whole(pltpu.HBM)] * 2,
        out_specs=whole(),
        scratch_shapes=[pltpu.SemaphoreType.DMA((2,))],
        compiler_params=limit(1),
        name="pack",
        cost_estimate=cost(SPAN * HD, 8 * SPAN * HD),
    )(keys, values)


NEAR_A = (0, -1, 1, 2)
FAR_B = (-1, 1, 2)
SLOTS = tuple((a, y, b) for y in (0, 1) for b in (0, *FAR_B) for a in NEAR_A)


def attend_kernel(other, arrays, order_ref, queries_ref, *refs):
    kv_refs, refs = refs[:arrays], refs[arrays:]
    out_ref, *refs = refs
    if arrays > 1:
        kv_ref, *refs = refs
        at = 0
        for ref in kv_refs:
            kv_ref[at : at + ref.shape[0], :] = ref[...]
            at += ref.shape[0]
    else:
        kv_ref = kv_refs[0]
    q_ref, s_ref, top_ref, m_ref, acc_ref, list_ref, kind_ref = refs

    row, col = lax.axis_index("row"), lax.axis_index("col")
    z, y, x, core = row >> 1, row & 1, col >> 1, col & 1
    first = core == 0
    at_a, at_b = jnp.where(first, z, x), jnp.where(first, x, z)
    wide_a, wide_b = jnp.where(first, 2, 16), jnp.where(first, 16, 2)
    part_a = {a: ((at_a + a) & 3) * wide_a + core * 8 for a in NEAR_A}
    part_b = {b: ((at_b + b) & 3) * wide_b for b in (0, *FAR_B)}
    part_y = (y, 1 - y)
    mine = order_ref[row * 8 + x * 2 + (1 - core if other else core)]
    used = jnp.int32(0)
    for slot, (a, dy, b) in enumerate(SLOTS):
        theirs = order_ref[part_a[a] + part_b[b] + part_y[dy]]
        list_ref[used] = slot
        kind_ref[used] = jnp.where(theirs == mine, 0, -SPAN)
        used = used + (theirs <= mine).astype(jnp.int32)
    for extra in range(GROUP - 1):
        list_ref[used + extra] = 0
        kind_ref[used + extra] = SPAN
    total = (used + GROUP - 1) >> 2

    for head in range(HEADS):
        q = queries_ref[:, head * HD : (head + 1) * HD].astype(jnp.float32) * SCALE
        high = q.astype(jnp.bfloat16)
        rows = slice(head * SPAN, (head + 1) * SPAN)
        q_ref[rows, :HD] = high
        q_ref[rows, HD:] = (q - high.astype(jnp.float32)).astype(jnp.bfloat16)
    m_ref[...] = jnp.full((ROWS, HD), NEVER, jnp.float32)
    acc_ref[...] = jnp.zeros((ROWS, 2 * HD), jnp.float32)
    above = lax.broadcasted_iota(jnp.int32, (SPAN, SPAN), 0) - lax.broadcasted_iota(jnp.int32, (SPAN, SPAN), 1)

    def keys_of(step, columns):
        spans = [list_ref[step * GROUP + g] for g in range(GROUP)]
        parts = [kv_ref[pl.ds(pl.multiple_of(s * SPAN, SPAN), SPAN), columns] for s in spans]
        return jnp.concatenate(parts, axis=0)

    def score(step, half):
        k = keys_of(step, slice(0, HD))
        s = lax.dot_general(
            q_ref[...],
            jnp.concatenate([k, k], axis=1),
            (((1,), (1,)), ((), ())),
            preferred_element_type=jnp.float32,
        )
        tiles = []
        for g in range(GROUP):
            allowed = above >= kind_ref[step * GROUP + g]
            tile = s[:, g * SPAN : (g + 1) * SPAN].reshape(HEADS, SPAN, SPAN)
            tiles.append(jnp.where(allowed[None], tile, NEVER).reshape(ROWS, SPAN))
        s_ref[half] = jnp.concatenate(tiles, axis=1)
        top_ref[half] = functools.reduce(jnp.maximum, tiles)

    def absorb(step, half):
        old = m_ref[...]
        new = jnp.maximum(old, jnp.max(top_ref[half], axis=1, keepdims=True))
        fade = jnp.exp2(old - new)
        m_ref[...] = new
        weights = jnp.exp2(s_ref[half] - jnp.concatenate([new] * GROUP, axis=1)).astype(jnp.bfloat16)
        v = jnp.concatenate([keys_of(step, slice(HD, 2 * HD)), jnp.ones((BLOCK, HD), jnp.bfloat16)], axis=1)
        more = jnp.dot(weights, v, preferred_element_type=jnp.float32)
        acc_ref[...] = acc_ref[...] * jnp.concatenate([fade, fade], axis=1) + more

    @pl.when(total > 0)
    def _():
        score(0, 0)

        def two(pair, carry):
            step = 2 * pair
            score(step + 1, 1)
            absorb(step, 0)
            score(step + 2, 0)
            absorb(step + 1, 1)
            return carry

        lax.fori_loop(0, (total - 1) >> 1, two, 0)

        @pl.when(total % 2 == 1)
        def _():
            absorb(total - 1, 0)

        @pl.when(total % 2 == 0)
        def _():
            score(total - 1, 1)
            absorb(total - 2, 0)
            absorb(total - 1, 1)

    low = lax.broadcasted_iota(jnp.int32, (ROWS, HD), 1) < HD // 2
    out_ref[:ROWS, :] = acc_ref[:, :HD]
    out_ref[ROWS:, :] = jnp.where(low, m_ref[...], acc_ref[:, HD:])


def attend(name, other, span_order, queries, arrays):
    count = len(SLOTS)
    out = [jax.ShapeDtypeStruct((2 * ROWS, HD), jnp.float32)]
    if len(arrays) > 1:
        out.append(jax.ShapeDtypeStruct((count * SPAN, 2 * HD), jnp.bfloat16))
    return pl.pallas_call(
        functools.partial(attend_kernel, other, len(arrays)),
        out_shape=out,
        in_specs=[whole(pltpu.SMEM)] + [whole()] * (1 + len(arrays)),
        out_specs=[whole()] * len(out),
        scratch_shapes=[
            VMEM((ROWS, 2 * HD), jnp.bfloat16),
            VMEM((2, ROWS, BLOCK), jnp.float32),
            VMEM((2, ROWS, HD), jnp.float32),
            VMEM((ROWS, HD), jnp.float32),
            VMEM((ROWS, 2 * HD), jnp.float32),
            pltpu.SMEM((count + GROUP,), jnp.int32),
            pltpu.SMEM((count + GROUP,), jnp.int32),
        ],
        compiler_params=limit(24),
        cost_estimate=cost(4 * count * ROWS * SPAN * HD, count * SPAN * SPAN * 4, count * ROWS * SPAN),
        name=name,
    )(span_order, queries, *arrays)


def merge_kernel(near_ref, far_ref, out_ref):
    low = lax.broadcasted_iota(jnp.int32, (SPAN, HD), 1) < HD // 2

    def spread(packed):
        turned = pltpu.roll(packed, HD // 2, 1)
        return jnp.where(low, packed, turned), jnp.where(low, turned, packed)

    for head in range(HEADS):
        rows = slice(head * SPAN, (head + 1) * SPAN)
        also = slice(ROWS + head * SPAN, ROWS + (head + 1) * SPAN)
        near, near_total = spread(near_ref[also, :])
        far, far_total = spread(far_ref[also, :])
        top = jnp.maximum(near, far)
        near, far = jnp.exp2(near - top), jnp.exp2(far - top)
        value = near_ref[rows, :] * near + far_ref[rows, :] * far
        out_ref[:, head * HD : (head + 1) * HD] = value / (near_total * near + far_total * far)


def merged(near, far):
    return pl.pallas_call(
        merge_kernel,
        out_shape=jax.ShapeDtypeStruct((SPAN, HEADS * HD), jnp.float32),
        in_specs=[whole()] * 2,
        out_specs=whole(),
        compiler_params=limit(8),
        name="merge",
        cost_estimate=cost(8 * ROWS * HD, 20 * ROWS * HD, 2 * ROWS * HD),
    )(near, far)


def local(queries, keys, values, span_order):
    kv = packed(keys, values)
    partner = send(queries, ACROSS_CORE)
    by_a = [send(kv, along_a(-d)) for d in NEAR_A[1:]]
    plane = jnp.concatenate([kv, *by_a], axis=0)
    other = send(plane, ACROSS_Y)
    by_b = [send(plane, along_b(-d)) for d in FAR_B]
    by_yb = [send(other, along_b(-d)) for d in FAR_B]
    arrays = [plane, *by_b, other, *by_yb]
    theirs, held = attend("attend_partner", True, span_order, partner, arrays)
    away = send(theirs, ACROSS_CORE)
    (mine,) = attend("attend_own", False, span_order, queries, [held])
    return merged(mine, away)


def solution(mesh):
    placed = (P(("row", "col"), "grp"), P(("col", "row"), "grp"), P(("col", "row"), "grp"), P())
    return jax.shard_map(
        local, mesh=mesh, in_specs=placed, out_specs=P(("row", "col"), "grp"), check_vma=False
    )
```

```python
import functools
import math

import jax
import jax.numpy as jnp
from jax import lax
from jax.experimental import pallas as pl
from jax.experimental.pallas import tpu as pltpu
from jax.sharding import PartitionSpec as P

HEADS = 8
HD = 128
SPAN = 128
ROWS = HEADS * SPAN
GROUP = 4
BLOCK = GROUP * SPAN
NEVER = -1e30
FLOOR = -1e29
SCALE = math.log2(math.e) / math.sqrt(HD)
VMEM = pltpu.VMEM
AXES = ("row", "col")


def place(z, y, x, core):
    return (z % 4 * 2 + y % 2) * 8 + x % 4 * 2 + core


def coords(index):
    row, col = divmod(index, 8)
    return row // 2, row % 2, col // 2, col % 2


def moved(to):
    return [(i, place(*to(*coords(i)))) for i in range(64)]


def along_a(step):
    return moved(lambda z, y, x, c: (z + step, y, x, c) if c == 0 else (z, y, x + step, c))


def along_b(step):
    return moved(lambda z, y, x, c: (z, y, x + step, c) if c == 0 else (z + step, y, x, c))


ACROSS_Y = moved(lambda z, y, x, c: (z, 1 - y, x, c))
ACROSS_CORE = moved(lambda z, y, x, c: (z, y, x, 1 - c))


def send(x, perm):
    return lax.ppermute(x, AXES, perm)


def whole(space=VMEM):
    return pl.BlockSpec(memory_space=space)


def limit(mib):
    return pltpu.CompilerParams(vmem_limit_bytes=mib << 20)


def cost(flops, moved_bytes, exps=0):
    return pl.CostEstimate(flops=flops, bytes_accessed=moved_bytes, transcendentals=exps)


NEAR_A = (0, -1, 1, 2)
FAR_B = (-1, 1, 2)
SLOTS = tuple((a, b) for b in (0, *FAR_B) for a in NEAR_A)
OWN, PARTNER, BESIDE, BESIDE_PARTNER = range(4)
NEAR = len(NEAR_A)
LISTS = (
    (OWN, 0, len(SLOTS)),
    (PARTNER, 0, len(SLOTS)),
    (BESIDE, NEAR, len(SLOTS)),
    (BESIDE_PARTNER, NEAR, len(SLOTS)),
    (BESIDE, 0, NEAR),
    (BESIDE_PARTNER, 0, NEAR),
)
KINDS = 32
STEPS = 63


def lists_kernel(order_ref, table_ref):
    row, col = lax.axis_index("row"), lax.axis_index("col")
    z, y, x, core = row >> 1, row & 1, col >> 1, col & 1
    first = core == 0
    at_a, at_b = jnp.where(first, z, x), jnp.where(first, x, z)
    wide_a, wide_b = jnp.where(first, 2, 16), jnp.where(first, 16, 2)
    part_a = {a: ((at_a + a) & 3) * wide_a + core * 8 + y for a in NEAR_A}
    part_b = {b: ((at_b + b) & 3) * wide_b for b in (0, *FAR_B)}
    theirs = [order_ref[part_a[a] + part_b[b]] for a, b in SLOTS]
    for u, (which, begin, end) in enumerate(LISTS):
        to_y = y if which < BESIDE else 1 - y
        to_core = core if which % 2 == 0 else 1 - core
        mine = order_ref[(z * 2 + to_y) * 8 + x * 2 + to_core]
        used = jnp.int32(0)
        for slot, order in list(enumerate(theirs))[begin:end]:
            table_ref[u, used] = slot
            table_ref[u, KINDS + used] = jnp.where(order == mine, 0, -SPAN)
            used = used + (order <= mine).astype(jnp.int32)
        for extra in range(GROUP):
            table_ref[u, used + extra] = begin
            table_ref[u, KINDS + used + extra] = SPAN
        table_ref[u, STEPS] = (used + GROUP - 1) >> 2


def lists(span_order):
    return pl.pallas_call(
        lists_kernel,
        out_shape=jax.ShapeDtypeStruct((len(LISTS), STEPS + 1), jnp.int32),
        in_specs=[whole(pltpu.SMEM)],
        out_specs=whole(pltpu.SMEM),
        compiler_params=limit(1),
        name="lists",
        cost_estimate=cost(1024, 1024),
    )(span_order)


def split_queries(queries_ref, q_ref):
    for head in range(HEADS):
        q = queries_ref[:, head * HD : (head + 1) * HD].astype(jnp.float32) * SCALE
        high = q.astype(jnp.bfloat16)
        rows = slice(head * SPAN, (head + 1) * SPAN)
        q_ref[rows, :HD] = high
        q_ref[rows, HD:] = (q - high.astype(jnp.float32)).astype(jnp.bfloat16)


def above_diagonal():
    return lax.broadcasted_iota(jnp.int32, (SPAN, SPAN), 0) - lax.broadcasted_iota(jnp.int32, (SPAN, SPAN), 1)


def keys_of(table_ref, u, kv_ref, step, columns):
    spans = [table_ref[u, step * GROUP + g] for g in range(GROUP)]
    parts = [kv_ref[pl.ds(pl.multiple_of(s * SPAN, SPAN), SPAN), columns] for s in spans]
    return jnp.concatenate(parts, axis=0)


def score_step(table_ref, u, kv_ref, q_ref, step, above, s_ref, top_ref):
    k = keys_of(table_ref, u, kv_ref, step, slice(0, HD))
    s = lax.dot_general(
        q_ref[...], jnp.concatenate([k, k], axis=1), (((1,), (1,)), ((), ())), preferred_element_type=jnp.float32
    )
    tiles = []
    for g in range(GROUP):
        allowed = above >= table_ref[u, KINDS + step * GROUP + g]
        tile = s[:, g * SPAN : (g + 1) * SPAN].reshape(HEADS, SPAN, SPAN)
        tiles.append(jnp.where(allowed[None], tile, NEVER).reshape(ROWS, SPAN))
    s_ref[...] = jnp.concatenate(tiles, axis=1)
    top_ref[...] = functools.reduce(jnp.maximum, tiles)


def absorb_step(table_ref, u, kv_ref, step, s_ref, top_ref, m_ref, acc_ref):
    old = m_ref[...]
    new = jnp.maximum(old, jnp.max(top_ref[...], axis=1, keepdims=True))
    fade = jnp.exp2(old - new)
    m_ref[...] = new
    weights = jnp.exp2(s_ref[...] - jnp.concatenate([new] * GROUP, axis=1)).astype(jnp.bfloat16)
    v = keys_of(table_ref, u, kv_ref, step, slice(HD, 2 * HD))
    v = jnp.concatenate([v, jnp.ones((BLOCK, HD), jnp.bfloat16)], axis=1)
    more = jnp.dot(weights, v, preferred_element_type=jnp.float32)
    acc_ref[...] = acc_ref[...] * jnp.concatenate([fade, fade], axis=1) + more


def near_kernel(lists_of, table_ref, *refs):
    count = len(lists_of)
    query_refs, kv_ref, refs = refs[:count], refs[count], refs[count + 1 :]
    m_refs, acc_refs, (q_ref, s_ref, top_ref) = refs[:count], refs[count : 2 * count], refs[2 * count :]
    above = above_diagonal()
    for i in range(count):
        split_queries(query_refs[i], q_ref.at[i])
        m_refs[i][...] = jnp.full((ROWS, HD), FLOOR, jnp.float32)
        acc_refs[i][...] = jnp.zeros((ROWS, 2 * HD), jnp.float32)
    for i, u in enumerate(lists_of):
        score_step(table_ref, u, kv_ref, q_ref.at[i], 0, above, s_ref.at[i], top_ref.at[i])
    for i, u in enumerate(lists_of):
        absorb_step(table_ref, u, kv_ref, 0, s_ref.at[i], top_ref.at[i], m_refs[i], acc_refs[i])


def attend_near(lists_of, table, queries, kv):
    count = len(lists_of)
    states = [jax.ShapeDtypeStruct((ROWS, HD), jnp.float32)] * count
    states += [jax.ShapeDtypeStruct((ROWS, 2 * HD), jnp.float32)] * count
    out = pl.pallas_call(
        functools.partial(near_kernel, lists_of),
        out_shape=states,
        in_specs=[whole(pltpu.SMEM)] + [whole()] * (count + 1),
        out_specs=[whole()] * (2 * count),
        scratch_shapes=[
            VMEM((count, ROWS, 2 * HD), jnp.bfloat16),
            VMEM((count, ROWS, BLOCK), jnp.float32),
            VMEM((count, ROWS, HD), jnp.float32),
        ],
        compiler_params=limit(24),
        cost_estimate=cost(4 * count * NEAR * ROWS * SPAN * HD, count * NEAR * SPAN * SPAN * 4, count * ROWS * BLOCK),
    )(table, *queries, kv)
    return list(zip(out[:count], out[count:]))


def attend_kernel(u, arrays, begun, table_ref, queries_ref, *refs):
    kv_refs, refs = refs[:arrays], refs[arrays:]
    if begun:
        m_in, acc_in, *refs = refs
    out_ref, *refs = refs
    if arrays > 1:
        kv_ref, *refs = refs
        at = 0
        for ref in kv_refs:
            kv_ref[at : at + ref.shape[0], :] = ref[...]
            at += ref.shape[0]
    else:
        kv_ref = kv_refs[0]
    q_ref, s_ref, top_ref, m_ref, acc_ref = refs
    total = table_ref[u, STEPS]

    split_queries(queries_ref, q_ref)
    if begun:
        m_ref[...] = m_in[...]
        acc_ref[...] = acc_in[...]
    else:
        m_ref[...] = jnp.full((ROWS, HD), FLOOR, jnp.float32)
        acc_ref[...] = jnp.zeros((ROWS, 2 * HD), jnp.float32)
    above = above_diagonal()

    def score(step, half):
        score_step(table_ref, u, kv_ref, q_ref, step, above, s_ref.at[half], top_ref.at[half])

    def absorb(step, half):
        absorb_step(table_ref, u, kv_ref, step, s_ref.at[half], top_ref.at[half], m_ref, acc_ref)

    @pl.when(total > 0)
    def _():
        score(0, 0)

        def two(pair, carry):
            step = 2 * pair
            score(step + 1, 1)
            absorb(step, 0)
            score(step + 2, 0)
            absorb(step + 1, 1)
            return carry

        lax.fori_loop(0, (total - 1) >> 1, two, 0)

        @pl.when(total % 2 == 1)
        def _():
            absorb(total - 1, 0)

        @pl.when(total % 2 == 0)
        def _():
            score(total - 1, 1)
            absorb(total - 2, 0)
            absorb(total - 1, 1)

    low = lax.broadcasted_iota(jnp.int32, (ROWS, HD), 1) < HD // 2
    out_ref[:ROWS, :] = acc_ref[:, :HD]
    out_ref[ROWS:, :] = jnp.where(low, m_ref[...], acc_ref[:, HD:])


def attend(u, table, queries, arrays, state=()):
    count = len(SLOTS)
    out = [jax.ShapeDtypeStruct((2 * ROWS, HD), jnp.float32)]
    if len(arrays) > 1:
        out.append(jax.ShapeDtypeStruct((count * SPAN, 2 * HD), jnp.bfloat16))
    return pl.pallas_call(
        functools.partial(attend_kernel, u, len(arrays), len(state) > 0),
        out_shape=out,
        in_specs=[whole(pltpu.SMEM)] + [whole()] * (1 + len(arrays) + len(state)),
        out_specs=[whole()] * len(out),
        scratch_shapes=[
            VMEM((ROWS, 2 * HD), jnp.bfloat16),
            VMEM((2, ROWS, BLOCK), jnp.float32),
            VMEM((2, ROWS, HD), jnp.float32),
            VMEM((ROWS, HD), jnp.float32),
            VMEM((ROWS, 2 * HD), jnp.float32),
        ],
        compiler_params=limit(24),
        cost_estimate=cost(4 * count * ROWS * SPAN * HD, count * SPAN * SPAN * 4, count * ROWS * SPAN),
    )(table, queries, *arrays, *state)


def lower_lanes():
    return lax.broadcasted_iota(jnp.int32, (SPAN, HD), 1) < HD // 2


def spread(packed):
    turned = pltpu.roll(packed, HD // 2, 1)
    low = lower_lanes()
    return jnp.where(low, packed, turned), jnp.where(low, turned, packed)


def join_kernel(near_ref, far_ref, out_ref):
    lane = lax.broadcasted_iota(jnp.int32, (SPAN, HD), 1)
    logs = jnp.zeros((SPAN, HD), jnp.bfloat16)
    for head in range(HEADS):
        rows = slice(head * SPAN, (head + 1) * SPAN)
        also = slice(ROWS + head * SPAN, ROWS + (head + 1) * SPAN)
        near, near_total = spread(near_ref[also, :])
        far, far_total = spread(far_ref[also, :])
        top = jnp.maximum(near, far)
        near, far = jnp.exp2(near - top), jnp.exp2(far - top)
        value = near_ref[rows, :] * near + far_ref[rows, :] * far
        weight = near_total * near + far_total * far
        live = weight > 0
        safe = jnp.where(live, weight, 1.0)
        out_ref[:, head * HD : (head + 1) * HD] = jnp.where(live, value / safe, 0.0).astype(jnp.bfloat16)
        rest = jnp.where(live, top + jnp.log(safe) * math.log2(math.e), NEVER)
        for part in range(3):
            piece = rest.astype(jnp.bfloat16)
            logs = jnp.where(lane == part * HEADS + head, piece, logs)
            rest = rest - piece.astype(jnp.float32)
    out_ref[:, HEADS * HD :] = logs


def joined(near, far):
    return pl.pallas_call(
        join_kernel,
        out_shape=jax.ShapeDtypeStruct((SPAN, (HEADS + 1) * HD), jnp.bfloat16),
        in_specs=[whole()] * 2,
        out_specs=whole(),
        compiler_params=limit(8),
        name="join",
        cost_estimate=cost(8 * ROWS * HD, 20 * ROWS * HD, 2 * ROWS * HD),
    )(near, far)


def merge_kernel(near_ref, far_ref, beside_ref, out_ref):
    parts = beside_ref[:, HEADS * HD :].astype(jnp.float32)
    logs = parts + pltpu.roll(parts, HD - HEADS, 1) + pltpu.roll(parts, HD - 2 * HEADS, 1)
    for head in range(HEADS):
        rows = slice(head * SPAN, (head + 1) * SPAN)
        also = slice(ROWS + head * SPAN, ROWS + (head + 1) * SPAN)
        columns = slice(head * HD, (head + 1) * HD)
        near, near_total = spread(near_ref[also, :])
        far, far_total = spread(far_ref[also, :])
        beside = jnp.broadcast_to(logs[:, head : head + 1], (SPAN, HD))
        top = jnp.maximum(jnp.maximum(near, far), beside)
        near, far, beside = jnp.exp2(near - top), jnp.exp2(far - top), jnp.exp2(beside - top)
        value = near_ref[rows, :] * near + far_ref[rows, :] * far + beside_ref[:, columns].astype(jnp.float32) * beside
        out_ref[:, columns] = value / (near_total * near + far_total * far + beside)


def merged(near, far, beside):
    return pl.pallas_call(
        merge_kernel,
        out_shape=jax.ShapeDtypeStruct((SPAN, HEADS * HD), jnp.float32),
        in_specs=[whole()] * 3,
        out_specs=whole(),
        compiler_params=limit(8),
        name="merge",
        cost_estimate=cost(8 * ROWS * HD, 20 * ROWS * HD, 2 * ROWS * HD),
    )(near, far, beside)


def together(keys, values):
    first = lax.broadcasted_iota(jnp.int32, (SPAN, 2 * HD), 1) < HD
    return jnp.where(first, jnp.pad(keys, ((0, 0), (0, HD))), jnp.pad(values, ((0, 0), (HD, 0))))


def attention(queries, keys, values, span_order):
    beside = send(queries, ACROSS_Y)
    kv = together(keys, values)
    by_a, by_b = {}, {}
    for d in (2, -1, 1):
        by_a[d] = send(kv, along_a(-d))
    table = lists(span_order)
    beside_partner = send(beside, ACROSS_CORE)
    plane = jnp.concatenate([kv, *(by_a[d] for d in NEAR_A[1:])], axis=0)
    for d in (2, -1, 1):
        by_b[d] = send(plane, along_b(-d))
    first, second = attend_near((5, 4), table, (beside_partner, beside), plane)
    partner = send(queries, ACROSS_CORE)

    arrays = [plane, *(by_b[d] for d in FAR_B)]
    far, held = attend(BESIDE_PARTNER, table, beside_partner, arrays, first)
    far = send(far, ACROSS_CORE)
    (near,) = attend(BESIDE, table, beside, [held], second)
    back = send(joined(near, far), ACROSS_Y)
    (far,) = attend(PARTNER, table, partner, [held])
    far = send(far, ACROSS_CORE)
    (near,) = attend(OWN, table, queries, [held])
    return merged(near, far, back)


def solution(mesh):
    placed = (P(("row", "col"), "grp"), P(("col", "row"), "grp"), P(("col", "row"), "grp"), P())
    return jax.shard_map(attention, mesh=mesh, in_specs=placed, out_specs=P(("row", "col"), "grp"), check_vma=False)
```

```python
import functools
import math

import jax
import jax.numpy as jnp
from jax import lax
from jax.experimental import pallas as pl
from jax.experimental.pallas import tpu as pltpu
from jax.sharding import PartitionSpec as P

HEADS = 8
HD = 128
SPAN = 128
ROWS = HEADS * SPAN
GROUP = 4
BLOCK = GROUP * SPAN
NEVER = -1e30
FLOOR = -1e29
SCALE = math.log2(math.e) / math.sqrt(HD)
VMEM = pltpu.VMEM
AXES = ("row", "col")


def place(z, y, x, core):
    return (z % 4 * 2 + y % 2) * 8 + x % 4 * 2 + core


def coords(index):
    row, col = divmod(index, 8)
    return row // 2, row % 2, col // 2, col % 2


def moved(to):
    return [(i, place(*to(*coords(i)))) for i in range(64)]


def along_a(step):
    return moved(lambda z, y, x, c: (z + step, y, x, c) if c == 0 else (z, y, x + step, c))


def along_b(step):
    return moved(lambda z, y, x, c: (z, y, x + step, c) if c == 0 else (z + step, y, x, c))


ACROSS_Y = moved(lambda z, y, x, c: (z, 1 - y, x, c))
ACROSS_CORE = moved(lambda z, y, x, c: (z, y, x, 1 - c))


def send(x, perm):
    return lax.ppermute(x, AXES, perm)


def whole(space=VMEM):
    return pl.BlockSpec(memory_space=space)


def limit(mib):
    return pltpu.CompilerParams(vmem_limit_bytes=mib << 20)


def cost(flops, moved_bytes, exps=0):
    return pl.CostEstimate(flops=flops, bytes_accessed=moved_bytes, transcendentals=exps)


NEAR_A = (0, -1, 1, 2)
FAR_B = (-1, 1, 2)
SLOTS = tuple((a, b) for b in (0, *FAR_B) for a in NEAR_A)
OWN, PARTNER, BESIDE, BESIDE_PARTNER = range(4)
NEAR = len(NEAR_A)
LISTS = (
    (OWN, 0, len(SLOTS)),
    (PARTNER, 0, len(SLOTS)),
    (BESIDE, NEAR, 3 * NEAR),
    (BESIDE_PARTNER, NEAR, 3 * NEAR),
    (BESIDE, 0, NEAR),
    (BESIDE_PARTNER, 0, NEAR),
    (BESIDE, 3 * NEAR, len(SLOTS)),
    (BESIDE_PARTNER, 3 * NEAR, len(SLOTS)),
)
KINDS = 32
STEPS = 63


def lists_kernel(order_ref, table_ref):
    row, col = lax.axis_index("row"), lax.axis_index("col")
    z, y, x, core = row >> 1, row & 1, col >> 1, col & 1
    first = core == 0
    at_a, at_b = jnp.where(first, z, x), jnp.where(first, x, z)
    wide_a, wide_b = jnp.where(first, 2, 16), jnp.where(first, 16, 2)
    part_a = {a: ((at_a + a) & 3) * wide_a + core * 8 + y for a in NEAR_A}
    part_b = {b: ((at_b + b) & 3) * wide_b for b in (0, *FAR_B)}
    theirs = [order_ref[part_a[a] + part_b[b]] for a, b in SLOTS]
    for u, (which, begin, end) in enumerate(LISTS):
        to_y = y if which < BESIDE else 1 - y
        to_core = core if which % 2 == 0 else 1 - core
        mine = order_ref[(z * 2 + to_y) * 8 + x * 2 + to_core]
        used = jnp.int32(0)
        for slot, order in list(enumerate(theirs))[begin:end]:
            table_ref[u, used] = slot
            table_ref[u, KINDS + used] = jnp.where(order == mine, 0, -SPAN)
            used = used + (order <= mine).astype(jnp.int32)
        for extra in range(GROUP):
            table_ref[u, used + extra] = begin
            table_ref[u, KINDS + used + extra] = SPAN
        table_ref[u, STEPS] = (used + 1) >> 1


def lists(span_order):
    return pl.pallas_call(
        lists_kernel,
        out_shape=jax.ShapeDtypeStruct((len(LISTS), STEPS + 1), jnp.int32),
        in_specs=[whole(pltpu.SMEM)],
        out_specs=whole(pltpu.SMEM),
        compiler_params=limit(1),
        name="lists",
        cost_estimate=cost(1024, 1024),
    )(span_order)


def split_queries(queries_ref, q_ref):
    for head in range(HEADS):
        q = queries_ref[:, head * HD : (head + 1) * HD].astype(jnp.float32) * SCALE
        high = q.astype(jnp.bfloat16)
        rows = slice(head * SPAN, (head + 1) * SPAN)
        q_ref[rows, :HD] = high
        q_ref[rows, HD:] = (q - high.astype(jnp.float32)).astype(jnp.bfloat16)


def above_diagonal():
    return lax.broadcasted_iota(jnp.int32, (SPAN, SPAN), 0) - lax.broadcasted_iota(jnp.int32, (SPAN, SPAN), 1)


def keys_of(table_ref, u, kv_ref, step, columns, begin, size):
    spans = [table_ref[u, step * GROUP + g] - begin for g in range(size)]
    parts = [kv_ref[pl.ds(pl.multiple_of(s * SPAN, SPAN), SPAN), columns] for s in spans]
    return jnp.concatenate(parts, axis=0)


def score_step(table_ref, u, kv_ref, q_ref, step, above, s_ref, top_ref, begin=0, size=GROUP):
    k = keys_of(table_ref, u, kv_ref, step, slice(0, HD), begin, size)
    s = lax.dot_general(
        q_ref[...], jnp.concatenate([k, k], axis=1), (((1,), (1,)), ((), ())), preferred_element_type=jnp.float32
    )
    tiles = []
    for g in range(size):
        allowed = above >= table_ref[u, KINDS + step * GROUP + g]
        tile = s[:, g * SPAN : (g + 1) * SPAN].reshape(HEADS, SPAN, SPAN)
        tiles.append(jnp.where(allowed[None], tile, NEVER).reshape(ROWS, SPAN))
    s_ref[:, : size * SPAN] = jnp.concatenate(tiles, axis=1)
    top_ref[...] = functools.reduce(jnp.maximum, tiles)


def absorb_step(table_ref, u, kv_ref, step, s_ref, top_ref, m_ref, acc_ref, begin=0, size=GROUP):
    old = m_ref[...]
    new = jnp.maximum(old, jnp.max(top_ref[...], axis=1, keepdims=True))
    fade = jnp.exp2(old - new)
    m_ref[...] = new
    scores = s_ref[:, : size * SPAN]
    weights = jnp.exp2(scores - jnp.concatenate([new] * size, axis=1)).astype(jnp.bfloat16)
    v = keys_of(table_ref, u, kv_ref, step, slice(HD, 2 * HD), begin, size)
    v = jnp.concatenate([v, jnp.ones((size * SPAN, HD), jnp.bfloat16)], axis=1)
    more = jnp.dot(weights, v, preferred_element_type=jnp.float32)
    acc_ref[...] = acc_ref[...] * jnp.concatenate([fade, fade], axis=1) + more


def early_kernel(lists_of, begin, begun, table_ref, *refs):
    count = len(lists_of)
    query_refs, kv_ref, refs = refs[:count], refs[count], refs[count + 1 :]
    if begun:
        m_in, acc_in, refs = refs[:count], refs[count : 2 * count], refs[2 * count :]
    m_refs, acc_refs, refs = refs[:count], refs[count : 2 * count], refs[2 * count :]
    *q_refs, s_ref, top_ref = refs
    q_refs = query_refs if begun else refs[:count]
    above = above_diagonal()
    for i in range(count):
        if begun:
            m_refs[i][...] = m_in[i][...]
            acc_refs[i][...] = acc_in[i][...]
        else:
            split_queries(query_refs[i], q_refs[i])
            m_refs[i][...] = jnp.full((ROWS, HD), FLOOR, jnp.float32)
            acc_refs[i][...] = jnp.zeros((ROWS, 2 * HD), jnp.float32)
    for i, u in enumerate(lists_of):
        score_step(table_ref, u, kv_ref, q_refs[i], 0, above, s_ref.at[i], top_ref.at[i], begin)
    for i, u in enumerate(lists_of):
        absorb_step(table_ref, u, kv_ref, 0, s_ref.at[i], top_ref.at[i], m_refs[i], acc_refs[i], begin)


def attend_early(lists_of, begin, table, queries, kv, states=()):
    count = len(lists_of)
    held = [m for m, _ in states] + [acc for _, acc in states]
    out = [jax.ShapeDtypeStruct((ROWS, HD), jnp.float32)] * count
    out += [jax.ShapeDtypeStruct((ROWS, 2 * HD), jnp.float32)] * count
    if not held:
        out += [jax.ShapeDtypeStruct((ROWS, 2 * HD), jnp.bfloat16)] * count
    out = pl.pallas_call(
        functools.partial(early_kernel, lists_of, begin, len(held) > 0),
        out_shape=out,
        in_specs=[whole(pltpu.SMEM)] + [whole()] * (count + 1 + len(held)),
        out_specs=[whole()] * len(out),
        scratch_shapes=[VMEM((count, ROWS, BLOCK), jnp.float32), VMEM((count, ROWS, HD), jnp.float32)],
        compiler_params=limit(24),
        cost_estimate=cost(4 * count * NEAR * ROWS * SPAN * HD, count * NEAR * SPAN * SPAN * 4, count * ROWS * BLOCK),
    )(table, *queries, kv, *held)
    return list(zip(out[:count], out[count : 2 * count])), out[2 * count :]


def attend_kernel(u, arrays, begin, begun, table_ref, queries_ref, *refs):
    kv_refs, refs = refs[:arrays], refs[arrays:]
    if begun:
        m_in, acc_in, *refs = refs
    out_ref, *refs = refs
    if arrays > 1:
        kv_ref, *refs = refs
        at = 0
        for ref in kv_refs:
            kv_ref[at : at + ref.shape[0], :] = ref[...]
            at += ref.shape[0]
    else:
        kv_ref = kv_refs[0]
    halves = table_ref[u, STEPS]
    if begun:
        q_ref = queries_ref
        s_ref, top_ref, m_ref, acc_ref = refs
    else:
        q_ref, s_ref, top_ref, m_ref, acc_ref = refs
        split_queries(queries_ref, q_ref)
    if begun:
        m_ref[...] = m_in[...]
        acc_ref[...] = acc_in[...]
    else:
        m_ref[...] = jnp.full((ROWS, HD), FLOOR, jnp.float32)
        acc_ref[...] = jnp.zeros((ROWS, 2 * HD), jnp.float32)
    above = above_diagonal()

    def score(step, half, size=GROUP):
        score_step(table_ref, u, kv_ref, q_ref, step, above, s_ref.at[half], top_ref.at[half], begin, size)

    def absorb(step, half, size=GROUP):
        absorb_step(table_ref, u, kv_ref, step, s_ref.at[half], top_ref.at[half], m_ref, acc_ref, begin, size)

    if begun:
        @pl.when(halves == 1)
        def _():
            score(0, 0, 2)
            absorb(0, 0, 2)

        @pl.when(halves == 2)
        def _():
            score(0, 0)
            absorb(0, 0)

        for last, size in ((3, 2), (4, GROUP)):

            @pl.when(halves == last)
            def _(size=size):
                score(0, 0)
                score(1, 1, size)
                absorb(0, 0)
                absorb(1, 1, size)
    else:
        total = (halves + 1) >> 1

        @pl.when(total > 0)
        def _():
            score(0, 0)

            def two(pair, carry):
                step = 2 * pair
                score(step + 1, 1)
                absorb(step, 0)
                score(step + 2, 0)
                absorb(step + 1, 1)
                return carry

            lax.fori_loop(0, (total - 1) >> 1, two, 0)

            @pl.when(total % 2 == 1)
            def _():
                absorb(total - 1, 0)

            @pl.when(total % 2 == 0)
            def _():
                score(total - 1, 1)
                absorb(total - 2, 0)
                absorb(total - 1, 1)

    low = lax.broadcasted_iota(jnp.int32, (ROWS, HD), 1) < HD // 2
    out_ref[:ROWS, :] = acc_ref[:, :HD]
    out_ref[ROWS:, :] = jnp.where(low, m_ref[...], acc_ref[:, HD:])


def attend(u, table, queries, arrays, begin=0, state=()):
    count = sum(array.shape[0] for array in arrays) // SPAN
    out = [jax.ShapeDtypeStruct((2 * ROWS, HD), jnp.float32)]
    if len(arrays) > 1:
        out.append(jax.ShapeDtypeStruct((count * SPAN, 2 * HD), jnp.bfloat16))
    return pl.pallas_call(
        functools.partial(attend_kernel, u, len(arrays), begin, len(state) > 0),
        out_shape=out,
        in_specs=[whole(pltpu.SMEM)] + [whole()] * (1 + len(arrays) + len(state)),
        out_specs=[whole()] * len(out),
        scratch_shapes=([] if state else [VMEM((ROWS, 2 * HD), jnp.bfloat16)])
        + [
            VMEM((2, ROWS, BLOCK), jnp.float32),
            VMEM((2, ROWS, HD), jnp.float32),
            VMEM((ROWS, HD), jnp.float32),
            VMEM((ROWS, 2 * HD), jnp.float32),
        ],
        compiler_params=limit(24),
        cost_estimate=cost(4 * count * ROWS * SPAN * HD, count * SPAN * SPAN * 4, count * ROWS * SPAN),
    )(table, queries, *arrays, *state)


def lower_lanes():
    return lax.broadcasted_iota(jnp.int32, (SPAN, HD), 1) < HD // 2


def spread(packed):
    turned = pltpu.roll(packed, HD // 2, 1)
    low = lower_lanes()
    return jnp.where(low, packed, turned), jnp.where(low, turned, packed)


def join_kernel(near_ref, far_ref, out_ref):
    lane = lax.broadcasted_iota(jnp.int32, (SPAN, HD), 1)
    logs = jnp.zeros((SPAN, HD), jnp.bfloat16)
    for head in range(HEADS):
        rows = slice(head * SPAN, (head + 1) * SPAN)
        also = slice(ROWS + head * SPAN, ROWS + (head + 1) * SPAN)
        near, near_total = spread(near_ref[also, :])
        far, far_total = spread(far_ref[also, :])
        top = jnp.maximum(near, far)
        near, far = jnp.exp2(near - top), jnp.exp2(far - top)
        value = near_ref[rows, :] * near + far_ref[rows, :] * far
        weight = near_total * near + far_total * far
        live = weight > 0
        safe = jnp.where(live, weight, 1.0)
        out_ref[:, head * HD : (head + 1) * HD] = jnp.where(live, value / safe, 0.0).astype(jnp.bfloat16)
        rest = jnp.where(live, top + jnp.log(safe) * math.log2(math.e), NEVER)
        for part in range(3):
            piece = rest.astype(jnp.bfloat16)
            logs = jnp.where(lane == part * HEADS + head, piece, logs)
            rest = rest - piece.astype(jnp.float32)
    out_ref[:, HEADS * HD :] = logs


def joined(near, far):
    return pl.pallas_call(
        join_kernel,
        out_shape=jax.ShapeDtypeStruct((SPAN, (HEADS + 1) * HD), jnp.bfloat16),
        in_specs=[whole()] * 2,
        out_specs=whole(),
        compiler_params=limit(8),
        name="join",
        cost_estimate=cost(8 * ROWS * HD, 20 * ROWS * HD, 2 * ROWS * HD),
    )(near, far)


def meet_kernel(near_ref, far_ref, value_ref, log_ref):
    for head in range(HEADS):
        rows = slice(head * SPAN, (head + 1) * SPAN)
        also = slice(ROWS + head * SPAN, ROWS + (head + 1) * SPAN)
        near, near_total = spread(near_ref[also, :])
        far, far_total = spread(far_ref[also, :])
        top = jnp.maximum(near, far)
        near, far = jnp.exp2(near - top), jnp.exp2(far - top)
        value = near_ref[rows, :] * near + far_ref[rows, :] * far
        weight = near_total * near + far_total * far
        live = weight > 0
        safe = jnp.where(live, weight, 1.0)
        value_ref[rows, :] = jnp.where(live, value / safe, 0.0)
        log_ref[rows, :] = jnp.where(live, top + jnp.log(safe) * math.log2(math.e), NEVER)


def met(near, far):
    return pl.pallas_call(
        meet_kernel,
        out_shape=[jax.ShapeDtypeStruct((ROWS, HD), jnp.float32)] * 2,
        in_specs=[whole()] * 2,
        out_specs=[whole()] * 2,
        compiler_params=limit(8),
        name="meet",
        cost_estimate=cost(8 * ROWS * HD, 24 * ROWS * HD, 2 * ROWS * HD),
    )(near, far)


def merge_kernel(value_ref, log_ref, beside_ref, out_ref, block_ref, done):
    parts = beside_ref[:, HEADS * HD :].astype(jnp.float32)
    logs = parts + pltpu.roll(parts, HD - HEADS, 1) + pltpu.roll(parts, HD - 2 * HEADS, 1)
    copies = []
    for head in range(HEADS):
        rows = slice(head * SPAN, (head + 1) * SPAN)
        columns = slice(head * HD, (head + 1) * HD)
        near = log_ref[rows, :]
        far = jnp.broadcast_to(logs[:, head : head + 1], (SPAN, HD))
        top = jnp.maximum(near, far)
        near, far = jnp.exp2(near - top), jnp.exp2(far - top)
        value = value_ref[rows, :] * near + beside_ref[:, columns].astype(jnp.float32) * far
        block_ref[head] = value / (near + far)
        copies.append(pltpu.make_async_copy(block_ref.at[head], out_ref.at[:, columns], done.at[head]))
        copies[-1].start()
    for copy in copies:
        copy.wait()


def merged(value, log, beside):
    return pl.pallas_call(
        merge_kernel,
        out_shape=jax.ShapeDtypeStruct((SPAN, HEADS * HD), jnp.float32),
        in_specs=[whole()] * 3,
        out_specs=whole(pltpu.HBM),
        scratch_shapes=[VMEM((HEADS, SPAN, HD), jnp.float32), pltpu.SemaphoreType.DMA((HEADS,))],
        compiler_params=limit(8),
        name="merge",
        cost_estimate=cost(8 * ROWS * HD, 16 * ROWS * HD, 2 * ROWS * HD),
    )(value, log, beside)


def together(keys, values):
    first = lax.broadcasted_iota(jnp.int32, (SPAN, 2 * HD), 1) < HD
    return jnp.where(first, jnp.pad(keys, ((0, 0), (0, HD))), jnp.pad(values, ((0, 0), (HD, 0))))


def attention(queries, keys, values, span_order):
    beside = send(queries, ACROSS_Y)
    kv = together(keys, values)
    by_a, by_b = {}, {}
    for d in (2, -1, 1):
        by_a[d] = send(kv, along_a(-d))
    table = lists(span_order)
    partner = send(queries, ACROSS_CORE)
    beside_partner = send(beside, ACROSS_CORE)
    plane = jnp.concatenate([kv, *(by_a[d] for d in NEAR_A[1:])], axis=0)
    for d in (2, -1, 1):
        by_b[d] = send(plane, along_b(-d))
    states, split = attend_early((5, 4), 0, table, (beside_partner, beside), plane)
    (first, second), _ = attend_early((7, 6), 3 * NEAR, table, split, by_b[2], states)
    pair = [by_b[-1], by_b[1]]
    far, pair = attend(BESIDE_PARTNER, table, split[0], pair, NEAR, first)
    far = send(far, ACROSS_CORE)
    (near,) = attend(BESIDE, table, split[1], [pair], NEAR, second)
    back = send(joined(near, far), ACROSS_Y)
    far, held = attend(PARTNER, table, partner, [plane, pair, by_b[2]])
    far = send(far, ACROSS_CORE)
    (near,) = attend(OWN, table, queries, [held])
    value, log = met(near, far)
    return merged(value, log, back)


def solution(mesh):
    placed = (P(("row", "col"), "grp"), P(("col", "row"), "grp"), P(("col", "row"), "grp"), P())
    return jax.shard_map(attention, mesh=mesh, in_specs=placed, out_specs=P(("row", "col"), "grp"), check_vma=False)
```

```python
import functools
import math

import jax
import jax.numpy as jnp
from jax import lax
from jax.experimental import pallas as pl
from jax.experimental.pallas import tpu as pltpu
from jax.sharding import PartitionSpec as P

HEADS = 8
HD = 128
SPAN = 128
ROWS = HEADS * SPAN
GROUP = 4
BLOCK = GROUP * SPAN
NEVER = -1e30
FLOOR = -1e29
FRESH = ()
SCALE = math.log2(math.e) / math.sqrt(HD)
VMEM = pltpu.VMEM
AXES = ("row", "col")


def place(z, y, x, core):
    return (z % 4 * 2 + y % 2) * 8 + x % 4 * 2 + core


def coords(index):
    row, col = divmod(index, 8)
    return row // 2, row % 2, col // 2, col % 2


def moved(to):
    return [(i, place(*to(*coords(i)))) for i in range(64)]


def along_a(step):
    return moved(lambda z, y, x, c: (z + step, y, x, c) if c == 0 else (z, y, x + step, c))


def along_b(step):
    return moved(lambda z, y, x, c: (z, y, x + step, c) if c == 0 else (z + step, y, x, c))


ACROSS_Y = moved(lambda z, y, x, c: (z, 1 - y, x, c))
ACROSS_CORE = moved(lambda z, y, x, c: (z, y, x, 1 - c))


def send(x, perm):
    return lax.ppermute(x, AXES, perm)


def whole(space=VMEM):
    return pl.BlockSpec(memory_space=space)


def limit(mib):
    return pltpu.CompilerParams(vmem_limit_bytes=mib << 20)


def cost(flops, moved_bytes, exps=0):
    return pl.CostEstimate(flops=flops, bytes_accessed=moved_bytes, transcendentals=exps)


NEAR_A = (0, -1, 1, 2)
FAR_B = (-1, 1, 2)


def ring(core, b):
    return tuple((core, a, b) for a in NEAR_A)


OWN, BESIDE = range(2)
LISTS = (
    (BESIDE, ring(0, 0) + ring(1, 0)),
    (BESIDE, ring(0, 2)),
    (BESIDE, ring(1, 2) + ring(0, -1) + ring(0, 1)),
    (BESIDE, ring(1, -1) + ring(1, 1)),
    (OWN, ring(0, 0) + ring(1, 0) + ring(0, 2) + ring(1, 2) + ring(0, -1) + ring(0, 1) + ring(1, -1) + ring(1, 1)),
)
KINDS = 48
STEPS = 127
TABLE = 8


def lists_kernel(order_ref, table_ref):
    row, col = lax.axis_index("row"), lax.axis_index("col")
    z, y, x, core = row >> 1, row & 1, col >> 1, col & 1
    orders = {}
    for other in range(2):
        there = 1 - core if other else core
        first = there == 0
        at_a, at_b = jnp.where(first, z, x), jnp.where(first, x, z)
        wide_a, wide_b = jnp.where(first, 2, 16), jnp.where(first, 16, 2)
        part_a = {a: ((at_a + a) & 3) * wide_a + there * 8 + y for a in NEAR_A}
        part_b = {b: ((at_b + b) & 3) * wide_b for b in (0, *FAR_B)}
        for b in (0, *FAR_B):
            for a in NEAR_A:
                orders[other, a, b] = order_ref[part_a[a] + part_b[b]]
    for u, (which, slots) in enumerate(LISTS):
        to_y = y if which == OWN else 1 - y
        mine = order_ref[(z * 2 + to_y) * 8 + x * 2 + core]
        used = jnp.int32(0)
        for slot, at in enumerate(slots):
            table_ref[u, used] = slot
            table_ref[u, KINDS + used] = jnp.where(orders[at] == mine, 0, -SPAN)
            used = used + (orders[at] <= mine).astype(jnp.int32)
        for extra in range(GROUP):
            table_ref[u, used + extra] = 0
            table_ref[u, KINDS + used + extra] = SPAN
        table_ref[u, STEPS] = (used + 1) >> 1


def lists(span_order):
    return pl.pallas_call(
        lists_kernel,
        out_shape=jax.ShapeDtypeStruct((TABLE, STEPS + 1), jnp.int32),
        in_specs=[whole(pltpu.SMEM)],
        out_specs=whole(pltpu.SMEM),
        compiler_params=limit(1),
        name="lists",
        cost_estimate=cost(1024, 1024),
    )(span_order)


def split_queries(queries_ref, q_ref):
    for head in range(HEADS):
        q = queries_ref[:, head * HD : (head + 1) * HD].astype(jnp.float32) * SCALE
        high = q.astype(jnp.bfloat16)
        rows = slice(head * SPAN, (head + 1) * SPAN)
        q_ref[rows, :HD] = high
        q_ref[rows, HD:] = (q - high.astype(jnp.float32)).astype(jnp.bfloat16)


def above_diagonal():
    return lax.broadcasted_iota(jnp.int32, (SPAN, SPAN), 0) - lax.broadcasted_iota(jnp.int32, (SPAN, SPAN), 1)


def keys_of(table_ref, u, kv_ref, step, columns, size):
    spans = [table_ref[u, step * GROUP + g] for g in range(size)]
    parts = [kv_ref[pl.ds(pl.multiple_of(s * SPAN, SPAN), SPAN), columns] for s in spans]
    return jnp.concatenate(parts, axis=0)


def score_step(table_ref, u, kv_ref, q_ref, step, above, s_ref, top_ref, size=GROUP):
    k = keys_of(table_ref, u, kv_ref, step, slice(0, HD), size)
    s = lax.dot_general(
        q_ref[...], jnp.concatenate([k, k], axis=1), (((1,), (1,)), ((), ())), preferred_element_type=jnp.float32
    )
    tiles = []
    for g in range(size):
        allowed = above >= table_ref[u, KINDS + step * GROUP + g]
        tile = s[:, g * SPAN : (g + 1) * SPAN].reshape(HEADS, SPAN, SPAN)
        tiles.append(jnp.where(allowed[None], tile, NEVER).reshape(ROWS, SPAN))
    s_ref[:, : size * SPAN] = jnp.concatenate(tiles, axis=1)
    top_ref[...] = functools.reduce(jnp.maximum, tiles)


def absorb_step(table_ref, u, kv_ref, step, s_ref, top_ref, m_ref, acc_ref, size=GROUP, held=None):
    top = jnp.max(top_ref[...], axis=1, keepdims=True)
    if held is FRESH:
        new = jnp.broadcast_to(jnp.maximum(top, FLOOR), (ROWS, HD))
    else:
        m_old, acc_old = held or (m_ref, acc_ref)
        old = m_old[...]
        new = jnp.maximum(old, top)
        fade = jnp.exp2(old - new)
    m_ref[...] = new
    scores = s_ref[:, : size * SPAN]
    weights = jnp.exp2(scores - jnp.concatenate([new] * size, axis=1)).astype(jnp.bfloat16)
    v = keys_of(table_ref, u, kv_ref, step, slice(HD, 2 * HD), size)
    v = jnp.concatenate([v, jnp.ones((size * SPAN, HD), jnp.bfloat16)], axis=1)
    more = jnp.dot(weights, v, preferred_element_type=jnp.float32)
    if held is FRESH:
        acc_ref[...] = more
    else:
        acc_ref[...] = acc_old[...] * jnp.concatenate([fade, fade], axis=1) + more


def steps_of(halves, most, table_ref, u, kv_ref, q_ref, state, held, s_ref, top_ref):
    m_ref, acc_ref = state
    above = above_diagonal()

    def score(step, half, size=GROUP):
        score_step(table_ref, u, kv_ref, q_ref, step, above, s_ref.at[half], top_ref.at[half], size)

    def absorb(step, half, size=GROUP, held=None):
        absorb_step(table_ref, u, kv_ref, step, s_ref.at[half], top_ref.at[half], m_ref, acc_ref, size, held)

    def keep():
        if held is FRESH:
            m_ref[...] = jnp.full((ROWS, HD), FLOOR, jnp.float32)
            acc_ref[...] = jnp.zeros((ROWS, 2 * HD), jnp.float32)
        else:
            m_ref[...] = held[0][...]
            acc_ref[...] = held[1][...]

    @pl.when(halves == 1)
    def _():
        score(0, 0, 2)
        absorb(0, 0, 2, held)

    if most <= 4:
        pl.when(halves == 0)(keep)

        @pl.when(halves == 2)
        def _():
            score(0, 0)
            absorb(0, 0, GROUP, held)

        for last, size in ((3, 2), (4, GROUP)):
            if last > most:
                continue

            @pl.when(halves == last)
            def _(size=size):
                score(0, 0)
                score(1, 1, size)
                absorb(0, 0, GROUP, held)
                absorb(1, 1, size)

        return

    pl.when(halves != 1)(keep)
    full, short = halves >> 1, halves & 1

    @pl.when(full > 0)
    def _():
        score(0, 0)

        def two(pair, carry):
            step = 2 * pair
            score(step + 1, 1)
            absorb(step, 0)
            score(step + 2, 0)
            absorb(step + 1, 1)
            return carry

        lax.fori_loop(0, (full - 1) >> 1, two, 0)
        odd = (full & 1) == 1

        @pl.when(odd & (short == 0))
        def _():
            absorb(full - 1, 0)

        @pl.when(odd & (short == 1))
        def _():
            score(full, 1, 2)
            absorb(full - 1, 0)
            absorb(full, 1, 2)

        @pl.when((~odd) & (short == 0))
        def _():
            score(full - 1, 1)
            absorb(full - 2, 0)
            absorb(full - 1, 1)

        @pl.when((~odd) & (short == 1))
        def _():
            score(full - 1, 1)
            absorb(full - 2, 0)
            score(full, 0, 2)
            absorb(full - 1, 1)
            absorb(full, 0, 2)


def result_of(state, head):
    m_ref, acc_ref = state
    rows = slice(head * SPAN, (head + 1) * SPAN)
    weight = acc_ref[rows, HD:]
    live = weight > 0
    safe = jnp.where(live, weight, 1.0)
    value = jnp.where(live, acc_ref[rows, :HD] / safe, 0.0)
    return value, jnp.where(live, m_ref[rows, :] + jnp.log(safe) * math.log2(math.e), NEVER)


STATE, PACKET, RESULT = range(3)


def attend_kernel(u, arrays, begun, gives, table_ref, queries_ref, *refs):
    *refs, list_ref, listed = refs
    fetch = pltpu.make_async_copy(table_ref, list_ref, listed)
    fetch.start()
    kv_refs, refs = refs[:arrays], refs[arrays:]
    held = FRESH
    if begun:
        m_in, acc_in, *refs = refs
        held = (m_in, acc_in)
    if gives == STATE:
        m_ref, acc_ref, *refs = refs
    elif gives == PACKET:
        packet_ref, *refs = refs
    else:
        value_ref, log_ref, *refs = refs
    if begun:
        q_ref = queries_ref
    else:
        q_ref, *refs = refs
        split_queries(queries_ref, q_ref)
    if gives != STATE:
        m_ref, acc_ref, *refs = refs
    if arrays > 1:
        kv_ref, *refs = refs
        at = 0
        for ref in kv_refs:
            kv_ref[at : at + ref.shape[0], :] = ref[...]
            at += ref.shape[0]
    else:
        kv_ref = kv_refs[0]
    s_ref, top_ref = refs
    state = (m_ref, acc_ref)
    most = len(LISTS[u][1]) // 2
    fetch.wait()
    steps_of(list_ref[u, STEPS], most, list_ref, u, kv_ref, q_ref, state, held, s_ref, top_ref)

    if gives == PACKET:
        lane = lax.broadcasted_iota(jnp.int32, (SPAN, HD), 1)
        logs = jnp.zeros((SPAN, HD), jnp.float32)
        for head in range(HEADS):
            value, rest = result_of(state, head)
            packet_ref[head * SPAN : (head + 1) * SPAN, :] = value.astype(jnp.bfloat16)
            for part in range(3):
                piece = rest.astype(jnp.bfloat16).astype(jnp.float32)
                logs = jnp.where(lane == part * HEADS + head, piece, logs)
                rest = rest - piece
        packet_ref[ROWS:, :] = logs.T[: 4 * HEADS, :].astype(jnp.bfloat16)
    elif gives == RESULT:
        for head in range(HEADS):
            rows = slice(head * SPAN, (head + 1) * SPAN)
            value_ref[rows, :], log_ref[rows, :] = result_of(state, head)


def attend(u, gives, table, queries, arrays, state=()):
    count = len(LISTS[u][1])
    maxima = jax.ShapeDtypeStruct((ROWS, HD), jnp.float32)
    sums = jax.ShapeDtypeStruct((ROWS, 2 * HD), jnp.float32)
    split = jax.ShapeDtypeStruct((ROWS, 2 * HD), jnp.bfloat16)
    out = {
        STATE: [maxima, sums],
        PACKET: [jax.ShapeDtypeStruct((ROWS + 4 * HEADS, HD), jnp.bfloat16)],
        RESULT: [maxima, maxima],
    }[gives]
    scratch = []
    if not state:
        if gives == STATE:
            out = [*out, split]
        else:
            scratch.append(VMEM(split.shape, split.dtype))
    if gives != STATE:
        scratch += [VMEM(maxima.shape, maxima.dtype), VMEM(sums.shape, sums.dtype)]
    if len(arrays) > 1:
        scratch.append(VMEM((count * SPAN, 2 * HD), jnp.bfloat16))
    scratch += [VMEM((2, ROWS, BLOCK), jnp.float32), VMEM((2, ROWS, HD), jnp.float32)]
    scratch += [pltpu.SMEM((TABLE, STEPS + 1), jnp.int32), pltpu.SemaphoreType.DMA]
    return pl.pallas_call(
        functools.partial(attend_kernel, u, len(arrays), len(state) > 0, gives),
        out_shape=out,
        in_specs=[whole()] * (2 + len(arrays) + len(state)),
        out_specs=[whole()] * len(out),
        scratch_shapes=scratch,
        compiler_params=limit(24),
        cost_estimate=cost(4 * count * ROWS * SPAN * HD, count * SPAN * SPAN * 4, count * ROWS * SPAN),
    )(table, queries, *arrays, *state)


def merge_kernel(value_ref, log_ref, beside_ref, out_ref, block_ref, done):
    parts = beside_ref[ROWS:, :].astype(jnp.float32)
    logs = parts[:HEADS, :] + parts[HEADS : 2 * HEADS, :] + parts[2 * HEADS : 3 * HEADS, :]
    logs = jnp.concatenate([logs] * (HD // HEADS), axis=0).T
    copies = []
    for head in range(HEADS):
        rows = slice(head * SPAN, (head + 1) * SPAN)
        columns = slice(head * HD, (head + 1) * HD)
        near = log_ref[rows, :]
        far = jnp.broadcast_to(logs[:, head : head + 1], (SPAN, HD))
        top = jnp.maximum(near, far)
        near, far = jnp.exp2(near - top), jnp.exp2(far - top)
        value = value_ref[rows, :] * near + beside_ref[rows, :].astype(jnp.float32) * far
        block_ref[head] = value / (near + far)
        copies.append(pltpu.make_async_copy(block_ref.at[head], out_ref.at[:, columns], done.at[head]))
        copies[-1].start()
    for copy in copies:
        copy.wait()


def merged(value, log, beside):
    return pl.pallas_call(
        merge_kernel,
        out_shape=jax.ShapeDtypeStruct((SPAN, HEADS * HD), jnp.float32),
        in_specs=[whole()] * 3,
        out_specs=whole(pltpu.HBM),
        scratch_shapes=[VMEM((HEADS, SPAN, HD), jnp.float32), pltpu.SemaphoreType.DMA((HEADS,))],
        compiler_params=limit(8),
        name="merge",
        cost_estimate=cost(8 * ROWS * HD, 16 * ROWS * HD, 2 * ROWS * HD),
    )(value, log, beside)


def together(keys, values):
    first = lax.broadcasted_iota(jnp.int32, (SPAN, 2 * HD), 1) < HD
    return jnp.where(first, jnp.pad(keys, ((0, 0), (0, HD))), jnp.pad(values, ((0, 0), (HD, 0))))


def attention(queries, keys, values, span_order):
    beside = send(queries, ACROSS_Y)
    kv = together(keys, values)
    by_a, by_b, also_b = {}, {}, {}
    for d in (2, -1, 1):
        by_a[d] = send(kv, along_a(-d))
    table = lists(span_order)
    plane = jnp.concatenate([kv, *(by_a[d] for d in NEAR_A[1:])], axis=0)
    also_plane = send(plane, ACROSS_CORE)
    for d in (2, -1, 1):
        by_b[d] = send(plane, along_b(-d))
        also_b[d] = send(by_b[d], ACROSS_CORE)
    *state, split = attend(0, STATE, table, beside, [plane, also_plane])
    state = attend(1, STATE, table, split, [by_b[2]], state)
    state = attend(2, STATE, table, split, [also_b[2], by_b[-1], by_b[1]], state)
    (packet,) = attend(3, PACKET, table, split, [also_b[-1], also_b[1]], state)
    back = send(packet, ACROSS_Y)
    arrays = [plane, also_plane, by_b[2], also_b[2], by_b[-1], by_b[1], also_b[-1], also_b[1]]
    value, log = attend(4, RESULT, table, queries, arrays)
    return merged(value, log, back)


def solution(mesh):
    placed = (P(("row", "col"), "grp"), P(("col", "row"), "grp"), P(("col", "row"), "grp"), P())
    return jax.shard_map(
        attention, mesh=mesh, in_specs=placed, out_specs=P(("row", "col"), "grp"), check_vma=False
    )
```

```python
import functools
import math

import jax
import jax.numpy as jnp
from jax import lax
from jax.experimental import pallas as pl
from jax.experimental.pallas import tpu as pltpu
from jax.sharding import PartitionSpec as P

HEADS = 8
HD = 128
SPAN = 128
ROWS = HEADS * SPAN
GROUP = 4
BLOCK = GROUP * SPAN
NEVER = -1e30
FLOOR = -1e29
FRESH = ()
SCALE = math.log2(math.e) / math.sqrt(HD)
VMEM = pltpu.VMEM
AXES = ("row", "col")


def place(z, y, x, core):
    return (z % 4 * 2 + y % 2) * 8 + x % 4 * 2 + core


def coords(index):
    row, col = divmod(index, 8)
    return row // 2, row % 2, col // 2, col % 2


def moved(to):
    return [(i, place(*to(*coords(i)))) for i in range(64)]


def along_a(step):
    return moved(lambda z, y, x, c: (z + step, y, x, c) if c == 0 else (z, y, x + step, c))


def along_b(step):
    return moved(lambda z, y, x, c: (z, y, x + step, c) if c == 0 else (z + step, y, x, c))


ACROSS_Y = moved(lambda z, y, x, c: (z, 1 - y, x, c))
ACROSS_CORE = moved(lambda z, y, x, c: (z, y, x, 1 - c))


def send(x, perm):
    return lax.ppermute(x, AXES, perm)


def whole(space=VMEM):
    return pl.BlockSpec(memory_space=space)


def limit(mib):
    return pltpu.CompilerParams(vmem_limit_bytes=mib << 20)


def cost(flops, moved_bytes, exps=0):
    return pl.CostEstimate(flops=flops, bytes_accessed=moved_bytes, transcendentals=exps)


NEAR_A = (0, -1, 1, 2)
FAR_B = (-1, 1, 2)


def ring(core, b):
    return tuple((core, a, b) for a in NEAR_A)


OWN, BESIDE = range(2)
LISTS = (
    (BESIDE, ring(0, 0) + ring(1, 0)),
    (BESIDE, ring(0, 2)),
    (BESIDE, ring(1, 2) + ring(0, -1) + ring(0, 1)),
    (BESIDE, ring(1, -1) + ring(1, 1)),
    (OWN, ring(0, 0) + ring(1, 0) + ring(0, 2) + ring(1, 2) + ring(0, -1) + ring(0, 1) + ring(1, -1) + ring(1, 1)),
)
KINDS = 48
STEPS = 127
TABLE = 8


def lists_kernel(order_ref, table_ref):
    row, col = lax.axis_index("row"), lax.axis_index("col")
    z, y, x, core = row >> 1, row & 1, col >> 1, col & 1
    orders = {}
    for other in range(2):
        there = 1 - core if other else core
        first = there == 0
        at_a, at_b = jnp.where(first, z, x), jnp.where(first, x, z)
        wide_a, wide_b = jnp.where(first, 2, 16), jnp.where(first, 16, 2)
        part_a = {a: ((at_a + a) & 3) * wide_a + there * 8 + y for a in NEAR_A}
        part_b = {b: ((at_b + b) & 3) * wide_b for b in (0, *FAR_B)}
        for b in (0, *FAR_B):
            for a in NEAR_A:
                orders[other, a, b] = order_ref[part_a[a] + part_b[b]]
    for u, (which, slots) in enumerate(LISTS):
        to_y = y if which == OWN else 1 - y
        mine = order_ref[(z * 2 + to_y) * 8 + x * 2 + core]
        used = jnp.int32(0)
        for slot, at in enumerate(slots):
            table_ref[u, used] = slot
            table_ref[u, KINDS + used] = jnp.where(orders[at] == mine, 0, -SPAN)
            used = used + (orders[at] <= mine).astype(jnp.int32)
        for extra in range(GROUP):
            table_ref[u, used + extra] = 0
            table_ref[u, KINDS + used + extra] = SPAN
        table_ref[u, STEPS] = (used + 1) >> 1


def lists(span_order):
    return pl.pallas_call(
        lists_kernel,
        out_shape=jax.ShapeDtypeStruct((TABLE, STEPS + 1), jnp.int32),
        in_specs=[whole(pltpu.SMEM)],
        out_specs=whole(pltpu.SMEM),
        compiler_params=limit(1),
        name="lists",
        cost_estimate=cost(1024, 1024),
    )(span_order)


def split_queries(queries_ref, q_ref):
    for head in range(HEADS):
        q = queries_ref[:, head * HD : (head + 1) * HD].astype(jnp.float32) * SCALE
        high = q.astype(jnp.bfloat16)
        rows = slice(head * SPAN, (head + 1) * SPAN)
        q_ref[rows, :HD] = high
        q_ref[rows, HD:] = (q - high.astype(jnp.float32)).astype(jnp.bfloat16)


def above_diagonal():
    return lax.broadcasted_iota(jnp.int32, (SPAN, SPAN), 0) - lax.broadcasted_iota(jnp.int32, (SPAN, SPAN), 1)


def keys_of(table_ref, u, kv_ref, step, columns, size):
    spans = [table_ref[u, step * GROUP + g] for g in range(size)]
    parts = [kv_ref[pl.ds(pl.multiple_of(s * SPAN, SPAN), SPAN), columns] for s in spans]
    return jnp.concatenate(parts, axis=0)


def score_step(table_ref, u, kv_ref, q_ref, step, above, s_ref, top_ref, size=GROUP):
    k = keys_of(table_ref, u, kv_ref, step, slice(0, HD), size)
    s = lax.dot_general(
        q_ref[...], jnp.concatenate([k, k], axis=1), (((1,), (1,)), ((), ())), preferred_element_type=jnp.float32
    )
    tiles = []
    for g in range(size):
        allowed = above >= table_ref[u, KINDS + step * GROUP + g]
        tile = s[:, g * SPAN : (g + 1) * SPAN].reshape(HEADS, SPAN, SPAN)
        tiles.append(jnp.where(allowed[None], tile, NEVER).reshape(ROWS, SPAN))
    s_ref[:, : size * SPAN] = jnp.concatenate(tiles, axis=1)
    top_ref[...] = functools.reduce(jnp.maximum, tiles)


def absorb_step(table_ref, u, kv_ref, step, s_ref, top_ref, m_ref, acc_ref, size=GROUP, held=None):
    top = jnp.max(top_ref[...], axis=1, keepdims=True)
    if held is FRESH:
        new = jnp.broadcast_to(jnp.maximum(top, FLOOR), (ROWS, HD))
    else:
        m_old, acc_old = held or (m_ref, acc_ref)
        old = m_old[...]
        new = jnp.maximum(old, top)
        fade = jnp.exp2(old - new)
    m_ref[...] = new
    scores = s_ref[:, : size * SPAN]
    weights = jnp.exp2(scores - jnp.concatenate([new] * size, axis=1)).astype(jnp.bfloat16)
    v = keys_of(table_ref, u, kv_ref, step, slice(HD, 2 * HD), size)
    v = jnp.concatenate([v, jnp.ones((size * SPAN, HD), jnp.bfloat16)], axis=1)
    more = jnp.dot(weights, v, preferred_element_type=jnp.float32)
    if held is FRESH:
        acc_ref[...] = more
    else:
        acc_ref[...] = acc_old[...] * jnp.concatenate([fade, fade], axis=1) + more


def steps_of(halves, most, table_ref, u, kv_ref, q_ref, state, held, s_ref, top_ref):
    m_ref, acc_ref = state
    above = above_diagonal()

    def score(step, half, size=GROUP):
        score_step(table_ref, u, kv_ref, q_ref, step, above, s_ref.at[half], top_ref.at[half], size)

    def absorb(step, half, size=GROUP, held=None):
        absorb_step(table_ref, u, kv_ref, step, s_ref.at[half], top_ref.at[half], m_ref, acc_ref, size, held)

    def keep():
        if held is FRESH:
            m_ref[...] = jnp.full((ROWS, HD), FLOOR, jnp.float32)
            acc_ref[...] = jnp.zeros((ROWS, 2 * HD), jnp.float32)
        else:
            m_ref[...] = held[0][...]
            acc_ref[...] = held[1][...]

    @pl.when(halves == 1)
    def _():
        score(0, 0, 2)
        absorb(0, 0, 2, held)

    if most <= 6:
        pl.when(halves == 0)(keep)
        for last in range(2, most + 1):
            sizes = [GROUP] * (last // 2) + [2] * (last % 2)

            @pl.when(halves == last)
            def _(sizes=sizes):
                score(0, 0, sizes[0])
                for step, size in enumerate(sizes):
                    if step + 1 < len(sizes):
                        score(step + 1, (step + 1) % 2, sizes[step + 1])
                    absorb(step, step % 2, size, held if step == 0 else None)

        return

    pl.when(halves != 1)(keep)
    full, short = halves >> 1, halves & 1

    @pl.when(full > 0)
    def _():
        score(0, 0)

        def two(pair, carry):
            step = 2 * pair
            score(step + 1, 1)
            absorb(step, 0)
            score(step + 2, 0)
            absorb(step + 1, 1)
            return carry

        lax.fori_loop(0, (full - 1) >> 1, two, 0)
        odd = (full & 1) == 1

        @pl.when(odd & (short == 0))
        def _():
            absorb(full - 1, 0)

        @pl.when(odd & (short == 1))
        def _():
            score(full, 1, 2)
            absorb(full - 1, 0)
            absorb(full, 1, 2)

        @pl.when((~odd) & (short == 0))
        def _():
            score(full - 1, 1)
            absorb(full - 2, 0)
            absorb(full - 1, 1)

        @pl.when((~odd) & (short == 1))
        def _():
            score(full - 1, 1)
            absorb(full - 2, 0)
            score(full, 0, 2)
            absorb(full - 1, 1)
            absorb(full, 0, 2)


def in_lanes(columns):
    lane = lax.broadcasted_iota(jnp.int32, (SPAN, HD), 1)
    out = jnp.zeros((SPAN, HD), jnp.float32)
    for head, column in enumerate(columns):
        out = jnp.where(lane == head, column, out)
    return out


def statistics(state):
    m_ref, acc_ref = state
    rows = [slice(head * SPAN, (head + 1) * SPAN) for head in range(HEADS)]
    return in_lanes([m_ref[r, :] for r in rows]), in_lanes([acc_ref[r, HD:] for r in rows])


def along_lanes(columns, head):
    return jnp.broadcast_to(columns[:, head : head + 1], (SPAN, HD))


STATE, PACKET, RESULT = range(3)


def attend_kernel(u, arrays, begun, gives, table_ref, queries_ref, *refs):
    *refs, list_ref, listed = refs
    fetch = pltpu.make_async_copy(table_ref, list_ref, listed)
    fetch.start()
    kv_refs, refs = refs[:arrays], refs[arrays:]
    held = FRESH
    if begun:
        m_in, acc_in, *refs = refs
        held = (m_in, acc_in)
    if gives == STATE:
        m_ref, acc_ref, *refs = refs
    elif gives == PACKET:
        packet_ref, *refs = refs
    else:
        sums_ref, stats_ref, *refs = refs
    if begun:
        q_ref = queries_ref
    else:
        q_ref, *refs = refs
        split_queries(queries_ref, q_ref)
    if gives != STATE:
        m_ref, acc_ref, *refs = refs
    if arrays > 1:
        kv_ref, *refs = refs
        at = 0
        for ref in kv_refs:
            kv_ref[at : at + ref.shape[0], :] = ref[...]
            at += ref.shape[0]
    else:
        kv_ref = kv_refs[0]
    s_ref, top_ref = refs
    state = (m_ref, acc_ref)
    most = len(LISTS[u][1]) // 2
    fetch.wait()
    steps_of(list_ref[u, STEPS], most, list_ref, u, kv_ref, q_ref, state, held, s_ref, top_ref)

    if gives == PACKET:
        top, weight = statistics(state)
        live = weight > 0
        safe = jnp.where(live, weight, 1.0)
        inverse = jnp.where(live, 1.0 / safe, 0.0)
        rest = jnp.where(live, top + jnp.log(safe) * math.log2(math.e), NEVER)
        lane = lax.broadcasted_iota(jnp.int32, (SPAN, HD), 1)
        rest = jnp.where(lane < HEADS, rest, 0.0)
        logs = jnp.zeros((SPAN, HD), jnp.float32)
        for part in range(3):
            piece = rest.astype(jnp.bfloat16).astype(jnp.float32)
            logs = logs + (pltpu.roll(piece, part * HEADS, 1) if part else piece)
            rest = rest - piece
        packet_ref[ROWS:, :] = logs.T[: 4 * HEADS, :].astype(jnp.bfloat16)
        for head in range(HEADS):
            rows = slice(head * SPAN, (head + 1) * SPAN)
            packet_ref[rows, :] = (acc_ref[rows, :HD] * along_lanes(inverse, head)).astype(jnp.bfloat16)
    elif gives == RESULT:
        top, weight = statistics(state)
        lane = lax.broadcasted_iota(jnp.int32, (SPAN, HD), 1)
        stats_ref[...] = jnp.where(lane < HEADS, top, pltpu.roll(weight, HEADS, 1))
        sums_ref[...] = acc_ref[:, :HD]


def attend(u, gives, table, queries, arrays, state=()):
    count = len(LISTS[u][1])
    maxima = jax.ShapeDtypeStruct((ROWS, HD), jnp.float32)
    sums = jax.ShapeDtypeStruct((ROWS, 2 * HD), jnp.float32)
    split = jax.ShapeDtypeStruct((ROWS, 2 * HD), jnp.bfloat16)
    out = {
        STATE: [maxima, sums],
        PACKET: [jax.ShapeDtypeStruct((ROWS + 4 * HEADS, HD), jnp.bfloat16)],
        RESULT: [maxima, jax.ShapeDtypeStruct((SPAN, HD), jnp.float32)],
    }[gives]
    scratch = []
    if not state:
        if gives == STATE:
            out = [*out, split]
        else:
            scratch.append(VMEM(split.shape, split.dtype))
    if gives != STATE:
        scratch += [VMEM(maxima.shape, maxima.dtype), VMEM(sums.shape, sums.dtype)]
    if len(arrays) > 1:
        scratch.append(VMEM((count * SPAN, 2 * HD), jnp.bfloat16))
    scratch += [VMEM((2, ROWS, BLOCK), jnp.float32), VMEM((2, ROWS, HD), jnp.float32)]
    scratch += [pltpu.SMEM((TABLE, STEPS + 1), jnp.int32), pltpu.SemaphoreType.DMA]
    return pl.pallas_call(
        functools.partial(attend_kernel, u, len(arrays), len(state) > 0, gives),
        out_shape=out,
        in_specs=[whole()] * (2 + len(arrays) + len(state)),
        out_specs=[whole()] * len(out),
        scratch_shapes=scratch,
        compiler_params=limit(24),
        cost_estimate=cost(4 * count * ROWS * SPAN * HD, count * SPAN * SPAN * 4, count * ROWS * SPAN),
    )(table, queries, *arrays, *state)


def merge_kernel(sums_ref, stats_ref, beside_ref, out_ref, block_ref, done):
    parts = beside_ref[ROWS:, :].astype(jnp.float32)
    far = parts[:HEADS, :] + parts[HEADS : 2 * HEADS, :] + parts[2 * HEADS : 3 * HEADS, :]
    far = jnp.concatenate([far] * (HD // HEADS), axis=0).T
    near = stats_ref[...]
    total = pltpu.roll(near, HD - HEADS, 1)
    top = jnp.maximum(near, far)
    near, far = jnp.exp2(near - top), jnp.exp2(far - top)
    total = total * near + far
    near, far = near / total, far / total
    copies = []
    for head in range(HEADS):
        rows = slice(head * SPAN, (head + 1) * SPAN)
        columns = slice(head * HD, (head + 1) * HD)
        value = sums_ref[rows, :] * along_lanes(near, head)
        block_ref[head] = value + beside_ref[rows, :].astype(jnp.float32) * along_lanes(far, head)
        copies.append(pltpu.make_async_copy(block_ref.at[head], out_ref.at[:, columns], done.at[head]))
        copies[-1].start()
    for copy in copies:
        copy.wait()


def merged(sums, stats, beside):
    return pl.pallas_call(
        merge_kernel,
        out_shape=jax.ShapeDtypeStruct((SPAN, HEADS * HD), jnp.float32),
        in_specs=[whole()] * 3,
        out_specs=whole(pltpu.HBM),
        scratch_shapes=[VMEM((HEADS, SPAN, HD), jnp.float32), pltpu.SemaphoreType.DMA((HEADS,))],
        compiler_params=limit(8),
        name="merge",
        cost_estimate=cost(8 * ROWS * HD, 16 * ROWS * HD, 2 * ROWS * HD),
    )(sums, stats, beside)


def together(keys, values):
    first = lax.broadcasted_iota(jnp.int32, (SPAN, 2 * HD), 1) < HD
    return jnp.where(first, jnp.pad(keys, ((0, 0), (0, HD))), jnp.pad(values, ((0, 0), (HD, 0))))


def attention(queries, keys, values, span_order):
    beside = send(queries, ACROSS_Y)
    kv = together(keys, values)
    by_a, by_b, also_b = {}, {}, {}
    for d in (2, -1, 1):
        by_a[d] = send(kv, along_a(-d))
    table = lists(span_order)
    plane = jnp.concatenate([kv, *(by_a[d] for d in NEAR_A[1:])], axis=0)
    also_plane = send(plane, ACROSS_CORE)
    for d in (2, -1, 1):
        by_b[d] = send(plane, along_b(-d))
        also_b[d] = send(by_b[d], ACROSS_CORE)
    *state, split = attend(0, STATE, table, beside, [plane, also_plane])
    state = attend(1, STATE, table, split, [by_b[2]], state)
    state = attend(2, STATE, table, split, [also_b[2], by_b[-1], by_b[1]], state)
    (packet,) = attend(3, PACKET, table, split, [also_b[-1], also_b[1]], state)
    back = send(packet, ACROSS_Y)
    arrays = [plane, also_plane, by_b[2], also_b[2], by_b[-1], by_b[1], also_b[-1], also_b[1]]
    sums, stats = attend(4, RESULT, table, queries, arrays)
    return merged(sums, stats, back)


def solution(mesh):
    placed = (P(("row", "col"), "grp"), P(("col", "row"), "grp"), P(("col", "row"), "grp"), P())
    return jax.shard_map(attention, mesh=mesh, in_specs=placed, out_specs=P(("row", "col"), "grp"), check_vma=False)
```

```python
import functools
import math

import jax
import jax.numpy as jnp
from jax import lax
from jax.experimental import pallas as pl
from jax.experimental.pallas import tpu as pltpu
from jax.sharding import PartitionSpec as P

HEADS = 8
HD = 128
SPAN = 128
ROWS = HEADS * SPAN
GROUP = 4
BLOCK = GROUP * SPAN
NEVER = -1e30
FLOOR = -1e29
FRESH = ()
SCALE = math.log2(math.e) / math.sqrt(HD)
VMEM = pltpu.VMEM
AXES = ("row", "col")


def place(z, y, x, core):
    return (z % 4 * 2 + y % 2) * 8 + x % 4 * 2 + core


def coords(index):
    row, col = divmod(index, 8)
    return row // 2, row % 2, col // 2, col % 2


def moved(to):
    return [(i, place(*to(*coords(i)))) for i in range(64)]


def along_a(step):
    return moved(lambda z, y, x, c: (z + step, y, x, c) if c == 0 else (z, y, x + step, c))


def along_b(step):
    return moved(lambda z, y, x, c: (z, y, x + step, c) if c == 0 else (z + step, y, x, c))


ACROSS_Y = moved(lambda z, y, x, c: (z, 1 - y, x, c))
ACROSS_CORE = moved(lambda z, y, x, c: (z, y, x, 1 - c))


def send(x, perm):
    return lax.ppermute(x, AXES, perm)


def whole(space=VMEM):
    return pl.BlockSpec(memory_space=space)


def limit(mib):
    return pltpu.CompilerParams(vmem_limit_bytes=mib << 20)


def cost(flops, moved_bytes, exps=0):
    return pl.CostEstimate(flops=flops, bytes_accessed=moved_bytes, transcendentals=exps)


NEAR_A = (0, -1, 1, 2)
FAR_B = (-1, 1, 2)


def ring(core, b):
    return tuple((core, a, b) for a in NEAR_A)


OWN, BESIDE = range(2)
LISTS = (
    (BESIDE, ring(0, 0) + ring(1, 0)),
    (BESIDE, ring(0, 2)),
    (BESIDE, ring(1, 2) + ring(0, -1) + ring(0, 1)),
    (BESIDE, ring(1, -1) + ring(1, 1)),
    (OWN, ring(0, 0) + ring(1, 0) + ring(0, 2) + ring(1, 2) + ring(0, -1) + ring(0, 1) + ring(1, -1) + ring(1, 1)),
)
KINDS = 48
STEPS = 127
TABLE = 8


def lists_kernel(order_ref, table_ref):
    row, col = lax.axis_index("row"), lax.axis_index("col")
    z, y, x, core = row >> 1, row & 1, col >> 1, col & 1
    orders = {}
    for other in range(2):
        there = 1 - core if other else core
        first = there == 0
        at_a, at_b = jnp.where(first, z, x), jnp.where(first, x, z)
        wide_a, wide_b = jnp.where(first, 2, 16), jnp.where(first, 16, 2)
        part_a = {a: ((at_a + a) & 3) * wide_a + there * 8 + y for a in NEAR_A}
        part_b = {b: ((at_b + b) & 3) * wide_b for b in (0, *FAR_B)}
        for b in (0, *FAR_B):
            for a in NEAR_A:
                orders[other, a, b] = order_ref[part_a[a] + part_b[b]]
    for u, (which, slots) in enumerate(LISTS):
        to_y = y if which == OWN else 1 - y
        mine = order_ref[(z * 2 + to_y) * 8 + x * 2 + core]
        used = jnp.int32(0)
        for slot, at in enumerate(slots):
            table_ref[u, used] = slot
            table_ref[u, KINDS + used] = jnp.where(orders[at] == mine, 0, -SPAN)
            used = used + (orders[at] <= mine).astype(jnp.int32)
        for extra in range(GROUP):
            table_ref[u, used + extra] = 0
            table_ref[u, KINDS + used + extra] = SPAN
        table_ref[u, STEPS] = (used + 1) >> 1


def lists(span_order):
    return pl.pallas_call(
        lists_kernel,
        out_shape=jax.ShapeDtypeStruct((TABLE, STEPS + 1), jnp.int32),
        in_specs=[whole(pltpu.SMEM)],
        out_specs=whole(pltpu.SMEM),
        compiler_params=limit(1),
        name="lists",
        cost_estimate=cost(1024, 1024),
    )(span_order)


def split_queries(queries_ref, q_ref):
    for head in range(HEADS):
        q = queries_ref[:, head * HD : (head + 1) * HD].astype(jnp.float32) * SCALE
        high = q.astype(jnp.bfloat16)
        rows = slice(head * SPAN, (head + 1) * SPAN)
        q_ref[rows, :HD] = high
        q_ref[rows, HD:] = (q - high.astype(jnp.float32)).astype(jnp.bfloat16)


def above_diagonal():
    return lax.broadcasted_iota(jnp.int32, (SPAN, SPAN), 0) - lax.broadcasted_iota(jnp.int32, (SPAN, SPAN), 1)


def keys_of(table_ref, u, kv_ref, step, columns, size):
    spans = [table_ref[u, step * GROUP + g] for g in range(size)]
    parts = [kv_ref[pl.ds(pl.multiple_of(s * SPAN, SPAN), SPAN), columns] for s in spans]
    return jnp.concatenate(parts, axis=0)


def score_step(table_ref, u, kv_ref, q_ref, step, above, s_ref, top_ref, size=GROUP):
    k = keys_of(table_ref, u, kv_ref, step, slice(0, HD), size)
    s = lax.dot_general(
        q_ref[...], jnp.concatenate([k, k], axis=1), (((1,), (1,)), ((), ())), preferred_element_type=jnp.float32
    )
    tiles = []
    for g in range(size):
        allowed = above >= table_ref[u, KINDS + step * GROUP + g]
        tile = s[:, g * SPAN : (g + 1) * SPAN].reshape(HEADS, SPAN, SPAN)
        tiles.append(jnp.where(allowed[None], tile, NEVER).reshape(ROWS, SPAN))
    s_ref[:, : size * SPAN] = jnp.concatenate(tiles, axis=1)
    top_ref[...] = functools.reduce(jnp.maximum, tiles)


def absorb_step(table_ref, u, kv_ref, step, s_ref, top_ref, m_ref, acc_ref, size=GROUP, held=None):
    top = jnp.max(top_ref[...], axis=1, keepdims=True)
    if held is FRESH:
        new = jnp.broadcast_to(jnp.maximum(top, FLOOR), (ROWS, HD))
    else:
        m_old, acc_old = held or (m_ref, acc_ref)
        old = m_old[...]
        new = jnp.maximum(old, top)
        fade = jnp.exp2(old - new)
    m_ref[...] = new
    scores = s_ref[:, : size * SPAN]
    weights = jnp.exp2(scores - jnp.concatenate([new] * size, axis=1)).astype(jnp.bfloat16)
    v = keys_of(table_ref, u, kv_ref, step, slice(HD, 2 * HD), size)
    v = jnp.concatenate([v, jnp.ones((size * SPAN, HD), jnp.bfloat16)], axis=1)
    more = jnp.dot(weights, v, preferred_element_type=jnp.float32)
    if held is FRESH:
        acc_ref[...] = more
    else:
        acc_ref[...] = acc_old[...] * jnp.concatenate([fade, fade], axis=1) + more


def steps_of(halves, most, table_ref, u, kv_ref, q_ref, state, held, s_ref, top_ref):
    m_ref, acc_ref = state
    above = above_diagonal()

    def score(step, half, size=GROUP):
        score_step(table_ref, u, kv_ref, q_ref, step, above, s_ref.at[half], top_ref.at[half], size)

    def absorb(step, half, size=GROUP, held=None):
        absorb_step(table_ref, u, kv_ref, step, s_ref.at[half], top_ref.at[half], m_ref, acc_ref, size, held)

    def keep():
        if held is FRESH:
            m_ref[...] = jnp.full((ROWS, HD), FLOOR, jnp.float32)
            acc_ref[...] = jnp.zeros((ROWS, 2 * HD), jnp.float32)
        else:
            m_ref[...] = held[0][...]
            acc_ref[...] = held[1][...]

    @pl.when(halves == 1)
    def _():
        score(0, 0, 2)
        absorb(0, 0, 2, held)

    if most <= 6:
        pl.when(halves == 0)(keep)
        for last in range(2, most + 1):
            sizes = [GROUP] * (last // 2) + [2] * (last % 2)

            @pl.when(halves == last)
            def _(sizes=sizes):
                score(0, 0, sizes[0])
                for step, size in enumerate(sizes):
                    if step + 1 < len(sizes):
                        score(step + 1, (step + 1) % 2, sizes[step + 1])
                    absorb(step, step % 2, size, held if step == 0 else None)

        return

    pl.when(halves != 1)(keep)
    full, short = halves >> 1, halves & 1

    @pl.when(full > 0)
    def _():
        score(0, 0)

        def two(pair, carry):
            step = 2 * pair
            score(step + 1, 1)
            absorb(step, 0)
            score(step + 2, 0)
            absorb(step + 1, 1)
            return carry

        lax.fori_loop(0, (full - 1) >> 1, two, 0)
        odd = (full & 1) == 1

        @pl.when(odd & (short == 0))
        def _():
            absorb(full - 1, 0)

        @pl.when(odd & (short == 1))
        def _():
            score(full, 1, 2)
            absorb(full - 1, 0)
            absorb(full, 1, 2)

        @pl.when((~odd) & (short == 0))
        def _():
            score(full - 1, 1)
            absorb(full - 2, 0)
            absorb(full - 1, 1)

        @pl.when((~odd) & (short == 1))
        def _():
            score(full - 1, 1)
            absorb(full - 2, 0)
            score(full, 0, 2)
            absorb(full - 1, 1)
            absorb(full, 0, 2)


def in_lanes(columns):
    lane = lax.broadcasted_iota(jnp.int32, (SPAN, HD), 1)
    out = jnp.zeros((SPAN, HD), jnp.float32)
    for head, column in enumerate(columns):
        out = jnp.where(lane == head, column, out)
    return out


def statistics(state):
    m_ref, acc_ref = state
    rows = [slice(head * SPAN, (head + 1) * SPAN) for head in range(HEADS)]
    return in_lanes([m_ref[r, :] for r in rows]), in_lanes([acc_ref[r, HD:] for r in rows])


def along_lanes(columns, head):
    return jnp.broadcast_to(columns[:, head : head + 1], (SPAN, HD))


STATE, PACKET, RESULT = range(3)


def attend_kernel(u, arrays, begun, gives, table_ref, queries_ref, *refs):
    *refs, list_ref, listed = refs
    fetch = pltpu.make_async_copy(table_ref, list_ref, listed)
    fetch.start()
    kv_refs, refs = refs[:arrays], refs[arrays:]
    held = FRESH
    if begun:
        m_in, acc_in, *refs = refs
        held = (m_in, acc_in)
    if gives == STATE:
        m_ref, acc_ref, *refs = refs
    elif gives == PACKET:
        packet_ref, *refs = refs
    else:
        sums_ref, stats_ref, *refs = refs
    if begun:
        q_ref = queries_ref
    else:
        q_ref, *refs = refs
        split_queries(queries_ref, q_ref)
    if gives != STATE:
        m_ref, acc_ref, *refs = refs
    if arrays > 1:
        kv_ref, *refs = refs
        at = 0
        for ref in kv_refs:
            kv_ref[at : at + ref.shape[0], :] = ref[...]
            at += ref.shape[0]
    else:
        kv_ref = kv_refs[0]
    s_ref, top_ref = refs
    state = (m_ref, acc_ref)
    most = len(LISTS[u][1]) // 2
    fetch.wait()
    steps_of(list_ref[u, STEPS], most, list_ref, u, kv_ref, q_ref, state, held, s_ref, top_ref)

    if gives == PACKET:
        top, weight = statistics(state)
        live = weight > 0
        safe = jnp.where(live, weight, 1.0)
        inverse = jnp.where(live, 1.0 / safe, 0.0)
        rest = jnp.where(live, top + jnp.log(safe) * math.log2(math.e), NEVER)
        lane = lax.broadcasted_iota(jnp.int32, (SPAN, HD), 1)
        rest = jnp.where(lane < HEADS, rest, 0.0)
        logs = jnp.zeros((SPAN, HD), jnp.float32)
        for part in range(3):
            piece = rest.astype(jnp.bfloat16).astype(jnp.float32)
            logs = logs + (pltpu.roll(piece, part * HEADS, 1) if part else piece)
            rest = rest - piece
        packet_ref[ROWS:, :] = logs.T[: 4 * HEADS, :].astype(jnp.bfloat16)
        for head in range(HEADS):
            rows = slice(head * SPAN, (head + 1) * SPAN)
            packet_ref[rows, :] = (acc_ref[rows, :HD] * along_lanes(inverse, head)).astype(jnp.bfloat16)
    elif gives == RESULT:
        top, weight = statistics(state)
        lane = lax.broadcasted_iota(jnp.int32, (SPAN, HD), 1)
        stats_ref[...] = jnp.where(lane < HEADS, top, pltpu.roll(weight, HEADS, 1))
        sums_ref[...] = acc_ref[:, :HD]


def attend(u, gives, table, queries, arrays, state=()):
    count = len(LISTS[u][1])
    maxima = jax.ShapeDtypeStruct((ROWS, HD), jnp.float32)
    sums = jax.ShapeDtypeStruct((ROWS, 2 * HD), jnp.float32)
    split = jax.ShapeDtypeStruct((ROWS, 2 * HD), jnp.bfloat16)
    out = {
        STATE: [maxima, sums],
        PACKET: [jax.ShapeDtypeStruct((ROWS + 4 * HEADS, HD), jnp.bfloat16)],
        RESULT: [maxima, jax.ShapeDtypeStruct((SPAN, HD), jnp.float32)],
    }[gives]
    scratch = []
    if not state:
        if gives == STATE:
            out = [*out, split]
        else:
            scratch.append(VMEM(split.shape, split.dtype))
    if gives != STATE:
        scratch += [VMEM(maxima.shape, maxima.dtype), VMEM(sums.shape, sums.dtype)]
    if len(arrays) > 1:
        scratch.append(VMEM((count * SPAN, 2 * HD), jnp.bfloat16))
    scratch += [VMEM((2, ROWS, BLOCK), jnp.float32), VMEM((2, ROWS, HD), jnp.float32)]
    scratch += [pltpu.SMEM((TABLE, STEPS + 1), jnp.int32), pltpu.SemaphoreType.DMA]
    return pl.pallas_call(
        functools.partial(attend_kernel, u, len(arrays), len(state) > 0, gives),
        out_shape=out,
        in_specs=[whole()] * (2 + len(arrays) + len(state)),
        out_specs=[whole()] * len(out),
        scratch_shapes=scratch,
        compiler_params=limit(24),
        cost_estimate=cost(4 * count * ROWS * SPAN * HD, count * SPAN * SPAN * 4, count * ROWS * SPAN),
    )(table, queries, *arrays, *state)


def merge_kernel(sums_ref, stats_ref, beside_ref, out_ref, block_ref, done):
    parts = beside_ref[ROWS:, :].astype(jnp.float32)
    far = parts[:HEADS, :] + parts[HEADS : 2 * HEADS, :] + parts[2 * HEADS : 3 * HEADS, :]
    far = jnp.concatenate([far] * (HD // HEADS), axis=0).T
    near = stats_ref[...]
    total = pltpu.roll(near, HD - HEADS, 1)
    top = jnp.maximum(near, far)
    near, far = jnp.exp2(near - top), jnp.exp2(far - top)
    total = total * near + far
    near, far = near / total, far / total
    copies = []
    for head in range(HEADS):
        rows = slice(head * SPAN, (head + 1) * SPAN)
        columns = slice(head * HD, (head + 1) * HD)
        value = sums_ref[rows, :] * along_lanes(near, head)
        block_ref[head] = value + beside_ref[rows, :].astype(jnp.float32) * along_lanes(far, head)
        copies.append(pltpu.make_async_copy(block_ref.at[head], out_ref.at[:, columns], done.at[head]))
        copies[-1].start()
    for copy in copies:
        copy.wait()


def merged(sums, stats, beside):
    return pl.pallas_call(
        merge_kernel,
        out_shape=jax.ShapeDtypeStruct((SPAN, HEADS * HD), jnp.float32),
        in_specs=[whole()] * 3,
        out_specs=whole(pltpu.HBM),
        scratch_shapes=[VMEM((HEADS, SPAN, HD), jnp.float32), pltpu.SemaphoreType.DMA((HEADS,))],
        compiler_params=limit(8),
        name="merge",
        cost_estimate=cost(8 * ROWS * HD, 16 * ROWS * HD, 2 * ROWS * HD),
    )(sums, stats, beside)


def together(keys, values):
    first = lax.broadcasted_iota(jnp.int32, (SPAN, 2 * HD), 1) < HD
    return jnp.where(first, jnp.pad(keys, ((0, 0), (0, HD))), jnp.pad(values, ((0, 0), (HD, 0))))


def attention(queries, keys, values, span_order):
    beside = send(queries, ACROSS_Y)
    kv = together(keys, values)
    by_a, by_b = {}, {}
    for d in (2, -1, 1):
        by_a[d] = send(kv, along_a(-d))
    table = lists(span_order)
    plane = jnp.concatenate([kv, *(by_a[d] for d in NEAR_A[1:])], axis=0)
    also_plane = send(plane, ACROSS_CORE)
    for d in (2, -1, 1):
        by_b[d] = send(plane, along_b(-d))
    also_far = send(by_b[2], ACROSS_CORE)
    sides = jnp.concatenate([by_b[-1], by_b[1]], axis=0)
    also_sides = send(sides, ACROSS_CORE)
    *state, split = attend(0, STATE, table, beside, [plane, also_plane])
    state = attend(1, STATE, table, split, [by_b[2]], state)
    state = attend(2, STATE, table, split, [also_far, sides], state)
    (packet,) = attend(3, PACKET, table, split, [also_sides], state)
    back = send(packet, ACROSS_Y)
    arrays = [plane, also_plane, by_b[2], also_far, sides, also_sides]
    sums, stats = attend(4, RESULT, table, queries, arrays)
    return merged(sums, stats, back)


def solution(mesh):
    placed = (P(("row", "col"), "grp"), P(("col", "row"), "grp"), P(("col", "row"), "grp"), P())
    return jax.shard_map(attention, mesh=mesh, in_specs=placed, out_specs=P(("row", "col"), "grp"), check_vma=False)
```

```python
import functools
import math

import jax
import jax.numpy as jnp
from jax import lax
from jax.experimental import pallas as pl
from jax.experimental.pallas import tpu as pltpu
from jax.sharding import PartitionSpec as P

HEADS = 8
HD = 128
SPAN = 128
ROWS = HEADS * SPAN
GROUP = 4
BLOCK = GROUP * SPAN
NEVER = -1e30
FLOOR = -1e29
FRESH = ()
SCALE = math.log2(math.e) / math.sqrt(HD)
VMEM = pltpu.VMEM
AXES = ("row", "col")


def place(z, y, x, core):
    return (z % 4 * 2 + y % 2) * 8 + x % 4 * 2 + core


def coords(index):
    row, col = divmod(index, 8)
    return row // 2, row % 2, col // 2, col % 2


def moved(to):
    return [(i, place(*to(*coords(i)))) for i in range(64)]


def along_a(step):
    return moved(lambda z, y, x, c: (z + step, y, x, c) if c == 0 else (z, y, x + step, c))


def along_b(step):
    return moved(lambda z, y, x, c: (z, y, x + step, c) if c == 0 else (z + step, y, x, c))


ACROSS_Y = moved(lambda z, y, x, c: (z, 1 - y, x, c))
ACROSS_CORE = moved(lambda z, y, x, c: (z, y, x, 1 - c))


def send(x, perm):
    return lax.ppermute(x, AXES, perm)


def whole(space=VMEM):
    return pl.BlockSpec(memory_space=space)


def limit(mib):
    return pltpu.CompilerParams(vmem_limit_bytes=mib << 20)


def cost(flops, moved_bytes, exps=0):
    return pl.CostEstimate(flops=flops, bytes_accessed=moved_bytes, transcendentals=exps)


NEAR_A = (0, -1, 1, 2)
FAR_B = (-1, 1, 2)


def ring(core, b):
    return tuple((core, a, b) for a in NEAR_A)


OWN, BESIDE = range(2)
LISTS = (
    (BESIDE, ring(0, 0)),
    (BESIDE, ring(1, 0) + ring(0, 2)),
    (BESIDE, ring(1, 2) + ring(0, -1) + ring(0, 1)),
    (BESIDE, ring(1, -1) + ring(1, 1)),
    (OWN, ring(0, 0) + ring(1, 0) + ring(0, 2) + ring(1, 2) + ring(0, -1) + ring(0, 1) + ring(1, -1) + ring(1, 1)),
)
KINDS = 48
STEPS = 127
TABLE = 8


def lists_kernel(order_ref, table_ref):
    row, col = lax.axis_index("row"), lax.axis_index("col")
    z, y, x, core = row >> 1, row & 1, col >> 1, col & 1
    orders = {}
    for other in range(2):
        there = 1 - core if other else core
        first = there == 0
        at_a, at_b = jnp.where(first, z, x), jnp.where(first, x, z)
        wide_a, wide_b = jnp.where(first, 2, 16), jnp.where(first, 16, 2)
        part_a = {a: ((at_a + a) & 3) * wide_a + there * 8 + y for a in NEAR_A}
        part_b = {b: ((at_b + b) & 3) * wide_b for b in (0, *FAR_B)}
        for b in (0, *FAR_B):
            for a in NEAR_A:
                orders[other, a, b] = order_ref[part_a[a] + part_b[b]]
    for u, (which, slots) in enumerate(LISTS):
        to_y = y if which == OWN else 1 - y
        mine = order_ref[(z * 2 + to_y) * 8 + x * 2 + core]
        used = jnp.int32(0)
        for slot, at in enumerate(slots):
            table_ref[u, used] = slot
            table_ref[u, KINDS + used] = jnp.where(orders[at] == mine, 0, -SPAN)
            used = used + (orders[at] <= mine).astype(jnp.int32)
        for extra in range(GROUP):
            table_ref[u, used + extra] = 0
            table_ref[u, KINDS + used + extra] = SPAN
        table_ref[u, STEPS] = (used + 1) >> 1


def lists(span_order):
    return pl.pallas_call(
        lists_kernel,
        out_shape=jax.ShapeDtypeStruct((TABLE, STEPS + 1), jnp.int32),
        in_specs=[whole(pltpu.SMEM)],
        out_specs=whole(pltpu.SMEM),
        compiler_params=limit(1),
        name="lists",
        cost_estimate=cost(1024, 1024),
    )(span_order)


def split_queries(queries_ref, q_ref):
    for head in range(HEADS):
        q = queries_ref[:, head * HD : (head + 1) * HD].astype(jnp.float32) * SCALE
        high = q.astype(jnp.bfloat16)
        rows = slice(head * SPAN, (head + 1) * SPAN)
        q_ref[rows, :HD] = high
        q_ref[rows, HD:] = (q - high.astype(jnp.float32)).astype(jnp.bfloat16)


def above_diagonal():
    return lax.broadcasted_iota(jnp.int32, (SPAN, SPAN), 0) - lax.broadcasted_iota(jnp.int32, (SPAN, SPAN), 1)


def keys_of(table_ref, u, kv_ref, step, columns, size):
    spans = [table_ref[u, step * GROUP + g] for g in range(size)]
    parts = [kv_ref[pl.ds(pl.multiple_of(s * SPAN, SPAN), SPAN), columns] for s in spans]
    return jnp.concatenate(parts, axis=0)


def score_step(table_ref, u, kv_ref, q_ref, step, above, s_ref, top_ref, size=GROUP):
    k = keys_of(table_ref, u, kv_ref, step, slice(0, HD), size)
    s = lax.dot_general(
        q_ref[...], jnp.concatenate([k, k], axis=1), (((1,), (1,)), ((), ())), preferred_element_type=jnp.float32
    )
    tiles = []
    for g in range(size):
        allowed = above >= table_ref[u, KINDS + step * GROUP + g]
        tile = s[:, g * SPAN : (g + 1) * SPAN].reshape(HEADS, SPAN, SPAN)
        tiles.append(jnp.where(allowed[None], tile, NEVER).reshape(ROWS, SPAN))
    s_ref[:, : size * SPAN] = jnp.concatenate(tiles, axis=1)
    top_ref[...] = functools.reduce(jnp.maximum, tiles)


def absorb_step(table_ref, u, kv_ref, step, s_ref, top_ref, m_ref, acc_ref, size=GROUP, held=None):
    top = jnp.max(top_ref[...], axis=1, keepdims=True)
    if held is FRESH:
        new = jnp.broadcast_to(jnp.maximum(top, FLOOR), (ROWS, HD))
    else:
        m_old, acc_old = held or (m_ref, acc_ref)
        old = m_old[...]
        new = jnp.maximum(old, top)
        fade = jnp.exp2(old - new)
    m_ref[...] = new
    scores = s_ref[:, : size * SPAN]
    weights = jnp.exp2(scores - jnp.concatenate([new] * size, axis=1)).astype(jnp.bfloat16)
    v = keys_of(table_ref, u, kv_ref, step, slice(HD, 2 * HD), size)
    v = jnp.concatenate([v, jnp.ones((size * SPAN, HD), jnp.bfloat16)], axis=1)
    more = jnp.dot(weights, v, preferred_element_type=jnp.float32)
    if held is FRESH:
        acc_ref[...] = more
    else:
        acc_ref[...] = acc_old[...] * jnp.concatenate([fade, fade], axis=1) + more


def steps_of(halves, most, table_ref, u, kv_ref, q_ref, state, held, s_ref, top_ref):
    m_ref, acc_ref = state
    above = above_diagonal()

    def score(step, half, size=GROUP):
        score_step(table_ref, u, kv_ref, q_ref, step, above, s_ref.at[half], top_ref.at[half], size)

    def absorb(step, half, size=GROUP, held=None):
        absorb_step(table_ref, u, kv_ref, step, s_ref.at[half], top_ref.at[half], m_ref, acc_ref, size, held)

    def keep():
        if held is FRESH:
            m_ref[...] = jnp.full((ROWS, HD), FLOOR, jnp.float32)
            acc_ref[...] = jnp.zeros((ROWS, 2 * HD), jnp.float32)
        else:
            m_ref[...] = held[0][...]
            acc_ref[...] = held[1][...]

    @pl.when(halves == 1)
    def _():
        score(0, 0, 2)
        absorb(0, 0, 2, held)

    if most <= 6:
        pl.when(halves == 0)(keep)
        for last in range(2, most + 1):
            sizes = [GROUP] * (last // 2) + [2] * (last % 2)

            @pl.when(halves == last)
            def _(sizes=sizes):
                score(0, 0, sizes[0])
                for step, size in enumerate(sizes):
                    if step + 1 < len(sizes):
                        score(step + 1, (step + 1) % 2, sizes[step + 1])
                    absorb(step, step % 2, size, held if step == 0 else None)

        return

    pl.when(halves != 1)(keep)
    full, short = halves >> 1, halves & 1

    @pl.when(full > 0)
    def _():
        score(0, 0)

        def two(pair, carry):
            step = 2 * pair
            score(step + 1, 1)
            absorb(step, 0)
            score(step + 2, 0)
            absorb(step + 1, 1)
            return carry

        lax.fori_loop(0, (full - 1) >> 1, two, 0)
        odd = (full & 1) == 1

        @pl.when(odd & (short == 0))
        def _():
            absorb(full - 1, 0)

        @pl.when(odd & (short == 1))
        def _():
            score(full, 1, 2)
            absorb(full - 1, 0)
            absorb(full, 1, 2)

        @pl.when((~odd) & (short == 0))
        def _():
            score(full - 1, 1)
            absorb(full - 2, 0)
            absorb(full - 1, 1)

        @pl.when((~odd) & (short == 1))
        def _():
            score(full - 1, 1)
            absorb(full - 2, 0)
            score(full, 0, 2)
            absorb(full - 1, 1)
            absorb(full, 0, 2)


def in_lanes(columns):
    lane = lax.broadcasted_iota(jnp.int32, (SPAN, HD), 1)
    out = jnp.zeros((SPAN, HD), jnp.float32)
    for head, column in enumerate(columns):
        out = jnp.where(lane == head, column, out)
    return out


def statistics(state):
    m_ref, acc_ref = state
    rows = [slice(head * SPAN, (head + 1) * SPAN) for head in range(HEADS)]
    return in_lanes([m_ref[r, :] for r in rows]), in_lanes([acc_ref[r, HD:] for r in rows])


def along_lanes(columns, head):
    return jnp.broadcast_to(columns[:, head : head + 1], (SPAN, HD))


STATE, PACKET, RESULT = range(3)


def attend_kernel(u, arrays, begun, gives, table_ref, queries_ref, *refs):
    *refs, list_ref, listed = refs
    fetch = pltpu.make_async_copy(table_ref, list_ref, listed)
    fetch.start()
    kv_refs, refs = refs[:arrays], refs[arrays:]
    held = FRESH
    if begun:
        m_in, acc_in, *refs = refs
        held = (m_in, acc_in)
    if gives == STATE:
        m_ref, acc_ref, *refs = refs
    elif gives == PACKET:
        packet_ref, *refs = refs
    else:
        sums_ref, stats_ref, *refs = refs
    if begun:
        q_ref = queries_ref
    else:
        q_ref, *refs = refs
        split_queries(queries_ref, q_ref)
    if gives != STATE:
        m_ref, acc_ref, *refs = refs
    if arrays > 1:
        kv_ref, *refs = refs
        at = 0
        for ref in kv_refs:
            kv_ref[at : at + ref.shape[0], :] = ref[...]
            at += ref.shape[0]
    else:
        kv_ref = kv_refs[0]
    s_ref, top_ref = refs
    state = (m_ref, acc_ref)
    most = len(LISTS[u][1]) // 2
    fetch.wait()
    steps_of(list_ref[u, STEPS], most, list_ref, u, kv_ref, q_ref, state, held, s_ref, top_ref)

    if gives == PACKET:
        top, weight = statistics(state)
        live = weight > 0
        safe = jnp.where(live, weight, 1.0)
        inverse = jnp.where(live, 1.0 / safe, 0.0)
        rest = jnp.where(live, top + jnp.log(safe) * math.log2(math.e), NEVER)
        lane = lax.broadcasted_iota(jnp.int32, (SPAN, HD), 1)
        rest = jnp.where(lane < HEADS, rest, 0.0)
        logs = jnp.zeros((SPAN, HD), jnp.float32)
        for part in range(3):
            piece = rest.astype(jnp.bfloat16).astype(jnp.float32)
            logs = logs + (pltpu.roll(piece, part * HEADS, 1) if part else piece)
            rest = rest - piece
        packet_ref[ROWS:, :] = logs.T[: 4 * HEADS, :].astype(jnp.bfloat16)
        for head in range(HEADS):
            rows = slice(head * SPAN, (head + 1) * SPAN)
            packet_ref[rows, :] = (acc_ref[rows, :HD] * along_lanes(inverse, head)).astype(jnp.bfloat16)
    elif gives == RESULT:
        top, weight = statistics(state)
        lane = lax.broadcasted_iota(jnp.int32, (SPAN, HD), 1)
        stats_ref[...] = jnp.where(lane < HEADS, top, pltpu.roll(weight, HEADS, 1))
        sums_ref[...] = acc_ref[:, :HD]


def attend(u, gives, table, queries, arrays, state=()):
    count = len(LISTS[u][1])
    maxima = jax.ShapeDtypeStruct((ROWS, HD), jnp.float32)
    sums = jax.ShapeDtypeStruct((ROWS, 2 * HD), jnp.float32)
    split = jax.ShapeDtypeStruct((ROWS, 2 * HD), jnp.bfloat16)
    out = {
        STATE: [maxima, sums],
        PACKET: [jax.ShapeDtypeStruct((ROWS + 4 * HEADS, HD), jnp.bfloat16)],
        RESULT: [maxima, jax.ShapeDtypeStruct((SPAN, HD), jnp.float32)],
    }[gives]
    scratch = []
    if not state:
        if gives == STATE:
            out = [*out, split]
        else:
            scratch.append(VMEM(split.shape, split.dtype))
    if gives != STATE:
        scratch += [VMEM(maxima.shape, maxima.dtype), VMEM(sums.shape, sums.dtype)]
    if len(arrays) > 1:
        scratch.append(VMEM((count * SPAN, 2 * HD), jnp.bfloat16))
    scratch += [VMEM((2, ROWS, BLOCK), jnp.float32), VMEM((2, ROWS, HD), jnp.float32)]
    scratch += [pltpu.SMEM((TABLE, STEPS + 1), jnp.int32), pltpu.SemaphoreType.DMA]
    return pl.pallas_call(
        functools.partial(attend_kernel, u, len(arrays), len(state) > 0, gives),
        out_shape=out,
        in_specs=[whole()] * (2 + len(arrays) + len(state)),
        out_specs=[whole()] * len(out),
        scratch_shapes=scratch,
        compiler_params=limit(24),
        cost_estimate=cost(4 * count * ROWS * SPAN * HD, count * SPAN * SPAN * 4, count * ROWS * SPAN),
    )(table, queries, *arrays, *state)


def merge_kernel(sums_ref, stats_ref, beside_ref, out_ref, block_ref, done):
    parts = beside_ref[ROWS:, :].astype(jnp.float32)
    far = parts[:HEADS, :] + parts[HEADS : 2 * HEADS, :] + parts[2 * HEADS : 3 * HEADS, :]
    far = jnp.concatenate([far] * (HD // HEADS), axis=0).T
    near = stats_ref[...]
    total = pltpu.roll(near, HD - HEADS, 1)
    top = jnp.maximum(near, far)
    near, far = jnp.exp2(near - top), jnp.exp2(far - top)
    total = total * near + far
    near, far = near / total, far / total
    copies = []
    for head in range(HEADS):
        rows = slice(head * SPAN, (head + 1) * SPAN)
        columns = slice(head * HD, (head + 1) * HD)
        value = sums_ref[rows, :] * along_lanes(near, head)
        block_ref[head] = value + beside_ref[rows, :].astype(jnp.float32) * along_lanes(far, head)
        copies.append(pltpu.make_async_copy(block_ref.at[head], out_ref.at[:, columns], done.at[head]))
        copies[-1].start()
    for copy in copies:
        copy.wait()


def merged(sums, stats, beside):
    return pl.pallas_call(
        merge_kernel,
        out_shape=jax.ShapeDtypeStruct((SPAN, HEADS * HD), jnp.float32),
        in_specs=[whole()] * 3,
        out_specs=whole(pltpu.HBM),
        scratch_shapes=[VMEM((HEADS, SPAN, HD), jnp.float32), pltpu.SemaphoreType.DMA((HEADS,))],
        compiler_params=limit(8),
        name="merge",
        cost_estimate=cost(8 * ROWS * HD, 16 * ROWS * HD, 2 * ROWS * HD),
    )(sums, stats, beside)


def together(keys, values):
    first = lax.broadcasted_iota(jnp.int32, (SPAN, 2 * HD), 1) < HD
    return jnp.where(first, jnp.pad(keys, ((0, 0), (0, HD))), jnp.pad(values, ((0, 0), (HD, 0))))


def attention(queries, keys, values, span_order):
    beside = send(queries, ACROSS_Y)
    kv = together(keys, values)
    by_a, by_b, also_b = {}, {}, {}
    for d in (2, -1, 1):
        by_a[d] = send(kv, along_a(-d))
    table = lists(span_order)
    plane = jnp.concatenate([kv, *(by_a[d] for d in NEAR_A[1:])], axis=0)
    also_plane = send(plane, ACROSS_CORE)
    for d in (2, -1, 1):
        by_b[d] = send(plane, along_b(-d))
        also_b[d] = send(by_b[d], ACROSS_CORE)
    *state, split = attend(0, STATE, table, beside, [plane])
    state = attend(1, STATE, table, split, [also_plane, by_b[2]], state)
    state = attend(2, STATE, table, split, [also_b[2], by_b[-1], by_b[1]], state)
    (packet,) = attend(3, PACKET, table, split, [also_b[-1], also_b[1]], state)
    back = send(packet, ACROSS_Y)
    arrays = [plane, also_plane, by_b[2], also_b[2], by_b[-1], by_b[1], also_b[-1], also_b[1]]
    sums, stats = attend(4, RESULT, table, queries, arrays)
    return merged(sums, stats, back)


def solution(mesh):
    placed = (P(("row", "col"), "grp"), P(("col", "row"), "grp"), P(("col", "row"), "grp"), P())
    return jax.shard_map(attention, mesh=mesh, in_specs=placed, out_specs=P(("row", "col"), "grp"), check_vma=False)
```
